128 devices in a mesh: leaf: 8 (over z, core), panel: 16 (over x, y).
Axes of the slice: x: 4, y: 4, z: 4, core: 2. Of those that a mesh axis runs over, the one named last changes fastest.
Arguments:
- pix_grand: int32 [512, 16], P(None, 'leaf'), may hold values from 0 to 255
- pix_mid: int32 [512, 4], replicated, may hold values from 0 to 255
- pix_root: int32 [512], replicated, may hold values from 0 to 255
- parent: int32 [16], P('leaf'), may hold values from 0 to 3
- emit_grand: float32 [16, 4096, 256], P('leaf', 'panel'), may hold values from -232 to -1
- emit_mid: float32 [4, 4096, 256], P(None, 'panel'), may hold values from -232 to -1
- emit_root: float32 [4096, 256], P('leaf'), may hold values from -12 to -1
- weight_grand: float32 [16, 4096, 4096], P('leaf', None, 'panel'), may hold values from 2.4414063e-05 to 0.00048828125
- root_middle_weight: float32 [4, 4096, 4096], P(None, 'leaf', 'panel'), may hold values from 2.4414063e-05 to 0.00048828125
- prior: float32 [4096], P('leaf'), may hold values from 2.4414063e-05 to 0.00048828125
Outputs:
- loglik: float32 [512], replicated
- flow_grand: float32 [16, 4096, 4096], P('leaf', None, 'panel')
- flow_mid: float32 [4, 4096, 4096], P(None, 'leaf', 'panel')
The draws below stay inside these ranges and needn't reach their ends.
All inputs are finite; a program needn't handle non-finite values.
Results may differ from the reference program's by a relative error of at most 0.0003.
Values sent between devices are 32-bit elements; how exact they have to be, the bound alone decides.
No kernel may reach another device: no remote copies, remote signals or barrier semaphores. Data moves between devices by JAX's collectives and lax.ppermute only.
A program may use at most 192 MiB of HBM per device.

```python
import math
import jax
import jax.numpy as jnp
from jax import lax

K = 4096
VALUES = 256
IMAGE_BATCH = 512
MID = 4
N_GRAND = 16
NODES = 21


def column_starts(key, count):
    perm_key, depth_key = jax.random.split(key, 2)
    row_keys = jax.random.split(perm_key, count)
    ranks = jax.vmap(lambda one_key: jax.random.permutation(one_key, VALUES))(row_keys)
    hits = max(1, VALUES // 16)
    chosen = ranks < hits
    depth = jax.random.uniform(depth_key, (count, VALUES), jnp.float32, 140.0, 220.0)
    return jnp.where(chosen, -depth, jnp.zeros_like(depth))


def coarse_partition(key, count):
    unit = jax.random.uniform(key, (count, K, VALUES), jnp.float32)
    return -1.0 - 11.0 * unit


def draw_emit_grand(key, part):
    base_key = jax.random.fold_in(key, 7101)
    coarse_random_key, offset_key = jax.random.split(base_key, 2)
    lookup_matrix = coarse_partition(coarse_random_key, N_GRAND) + column_starts(offset_key, N_GRAND)[:, None, :]
    return lookup_matrix.astype(jnp.float32)


def draw_emit_mid(key, part):
    base_key = jax.random.fold_in(key, 7202)
    coarse_random_key, offset_key = jax.random.split(base_key, 2)
    lookup_matrix = coarse_partition(coarse_random_key, MID) + column_starts(offset_key, MID)[:, None, :]
    return lookup_matrix.astype(jnp.float32)


def set_ends(drawn, rng, least, largest):
    longest = drawn.shape.index(max(drawn.shape))
    spots = []
    for shift in (0, 1):
        where = [jax.random.randint(jax.random.fold_in(rng, axis), (), 0, length) for axis, length in enumerate(drawn.shape)]
        where[longest] = (where[longest] + shift) % drawn.shape[longest]
        spots.append(tuple(where))
    return drawn.at[spots[0]].set(least).at[spots[1]].set(largest)


def block_levels(rng, dims, pieces, least, largest):
    level = 1.0
    for axis_at, parts in pieces:
        draws = jax.random.uniform(jax.random.fold_in(jax.random.fold_in(rng, 6), axis_at), (parts,), jnp.float32, least / len(pieces), largest / len(pieces))
        level = level * jnp.repeat(jnp.exp(draws), dims[axis_at] // parts).reshape((-1,) + (1,) * (len(dims) - 1 - axis_at))
    return level


def setup_inputs(seed: int = 0) -> dict:
    key_of = jax.random.split(jax.random.key(seed), 11)
    return {
        "pix_grand": set_ends(jax.random.randint(key_of[0], (IMAGE_BATCH, N_GRAND), 0, VALUES), jax.random.fold_in(key_of[0], 1), 0, VALUES - 1).astype(jnp.int32),
        "pix_mid": set_ends(jax.random.randint(key_of[1], (IMAGE_BATCH, MID), 0, VALUES), jax.random.fold_in(key_of[1], 1), 0, VALUES - 1).astype(jnp.int32),
        "pix_root": set_ends(jax.random.randint(key_of[2], (IMAGE_BATCH,), 0, VALUES), jax.random.fold_in(key_of[2], 1), 0, VALUES - 1).astype(jnp.int32),
        "parent": set_ends(jax.random.randint(key_of[3], (N_GRAND,), 0, MID), jax.random.fold_in(key_of[3], 1), 0, MID - 1).astype(jnp.int32),
        "emit_grand": draw_emit_grand(jax.random.fold_in(key_of[10], 71), 0),
        "emit_mid": draw_emit_mid(jax.random.fold_in(key_of[10], 71), 0),
        "emit_root": jnp.clip(-12.0 + 11.0 * jax.random.uniform(key_of[6], (K, VALUES), jnp.float32) ** block_levels(key_of[6], (K, VALUES), ((0, 8),), -0.2, 0.2), -12.0, -1.0),
        "weight_grand": jnp.clip(jnp.exp(math.log(0.00048828125) - 2.9957323 * jax.random.uniform(key_of[7], (N_GRAND, K, K), jnp.float32) ** block_levels(key_of[7], (N_GRAND, K, K), ((0, 8), (2, 16)), -0.2, 0.2)), 2.441406286379788e-05, 0.00048828125),
        "root_middle_weight": jnp.clip(jnp.exp(math.log(0.00048828125) - 2.9957323 * jax.random.uniform(key_of[8], (MID, K, K), jnp.float32) ** block_levels(key_of[8], (MID, K, K), ((1, 8), (2, 16)), -0.2, 0.2)), 2.441406286379788e-05, 0.00048828125),
        "prior": jnp.clip(jnp.exp(math.log(0.00048828125) - 2.9957323 * jax.random.uniform(key_of[9], (K,), jnp.float32) ** block_levels(key_of[9], (K,), ((0, 8),), -0.2, 0.2)), 2.441406286379788e-05, 0.00048828125),
    }


def reference(pix_grand, pix_mid, pix_root, parent, emit_grand, emit_mid, emit_root, weight_grand, root_middle_weight, prior):
    highest = lax.Precision.HIGHEST
    scale = (K * K) / IMAGE_BATCH

    def grand_up(index):
        lookup_matrix = emit_grand[index]
        potent = lookup_matrix[:, pix_grand[:, index]]
        upper = jnp.max(potent, axis=0)
        expo = jnp.exp(potent - upper[None, :])
        sums = jnp.dot(weight_grand[index], expo, precision=highest)
        return expo, sums, upper

    e_grand, grandchild_state_sum, top_grand = lax.map(grand_up, jnp.arange(N_GRAND, dtype=jnp.int32))
    m_grand = jnp.log(grandchild_state_sum) + top_grand[:, None, :]
    parent_hot = (parent[:, None] == jnp.arange(MID, dtype=jnp.int32)[None, :]).astype(jnp.float32)
    child_sum = jnp.einsum('gu,gkb->ukb', parent_hot, m_grand, precision=highest)
    a_mid = emit_mid[jnp.arange(MID, dtype=jnp.int32)[:, None, None], jnp.arange(K, dtype=jnp.int32)[None, :, None], jnp.transpose(pix_mid)[:, None, :]] + child_sum
    top_mid = jnp.max(a_mid, axis=1)
    e_mid = jnp.exp(a_mid - top_mid[:, None, :])
    s_mid = jnp.einsum('uij,ujb->uib', root_middle_weight, e_mid, precision=highest)
    m_mid = jnp.log(s_mid) + top_mid[:, None, :]
    scores = jnp.log(prior)[:, None] + emit_root[:, pix_root] + jnp.sum(m_mid, axis=0)
    top = jnp.max(scores, axis=0)
    expo_root = jnp.exp(scores - top[None, :])
    total = jnp.sum(expo_root, axis=0)
    loglik = (top + jnp.log(total)) / NODES
    q_root = expo_root / total[None, :]
    t_mid = q_root[None, :, :] / s_mid
    flow_mid = root_middle_weight * jnp.einsum('uib,ujb->uij', t_mid, e_mid, precision=highest) * scale
    q_mid = e_mid * jnp.einsum('uij,uib->ujb', root_middle_weight, t_mid, precision=highest)

    def grand_down(index):
        q_par = jnp.einsum('u,ukb->kb', parent_hot[index], q_mid, precision=highest)
        ratio = q_par / grandchild_state_sum[index]
        return weight_grand[index] * jnp.dot(ratio, jnp.transpose(e_grand[index]), precision=highest) * scale

    flow_grand = lax.map(grand_down, jnp.arange(N_GRAND, dtype=jnp.int32))
    return loglik, flow_grand, flow_mid
```

```python
import jax
import jax.numpy as jnp
from jax import lax
from jax.experimental import pallas as pl
from jax.experimental.pallas import tpu as pltpu
from jax.sharding import PartitionSpec as P


HIGH = lax.Precision.HIGH
HIGHEST = lax.Precision.HIGHEST
LIFT = 35.0
MEAN_W = 1.09e-4


def ring_x(d):
    return [(x * 4 + y, ((x + d) % 4) * 4 + y) for x in range(4) for y in range(4)]


def ring_y(d):
    return [(x * 4 + y, x * 4 + (y + d) % 4) for x in range(4) for y in range(4)]


def ring_z(d):
    return [(z * 2 + c, ((z + d) % 4) * 2 + c) for z in range(4) for c in range(2)]


def hop_leaf(d, flip):
    return [(z * 2 + c, ((z + d) % 4) * 2 + (c ^ flip)) for z in range(4) for c in range(2)]


def mover(axis, ring):
    return lambda v, d: lax.ppermute(v, axis, ring(d))


MOVE_X = mover("panel", ring_x)
MOVE_Y = mover("panel", ring_y)
MOVE_Z = mover("leaf", ring_z)


def ring_scatter(move, piece, scale=None, merged=True):
    if scale is None:
        scale = lambda v, d: v
        common = piece
    else:
        common = lambda d, h: piece(d, h, True)
    r1 = move(piece(2, 0), 1)
    r2 = move(piece(2, 1), -1)
    if merged:
        up = move(jnp.stack([common(1, 0) + scale(r1, -1), common(1, 1)]), 1)
        down = move(jnp.stack([common(-1, 0), common(-1, 1) + scale(r2, 1)]), -1)
        return common(0, 0) + up[0] + down[0], common(0, 1) + up[1] + down[1]
    r3 = move(piece(1, 1), 1)
    r4 = move(piece(-1, 0), -1)
    r5 = move(common(1, 0) + scale(r1, -1), 1)
    r6 = move(common(-1, 1) + scale(r2, 1), -1)
    return (
        common(0, 0) + scale(r4, 1) + r5,
        common(0, 1) + scale(r3, -1) + r6,
    )


def ring_gather(move, half0, half1, merged=True):
    if merged:
        both = jnp.stack([half0, half1])
        a, b = move(both, 1), move(both, -1)
        return {0: (half0, half1), -1: (a[0], a[1]), 1: (b[0], b[1]), 2: (move(a[0], 1), move(b[1], -1))}
    a1 = move(half0, 1)
    b2 = move(half1, -1)
    b1 = move(half1, 1)
    a2 = move(half0, -1)
    a3 = move(a1, 1)
    b3 = move(b2, -1)
    return {0: (half0, half1), -1: (a1, b1), 1: (a2, b2), 2: (a3, b3)}


def prepare(emit_grand, emit_mid):
    groups, width, values = emit_grand.shape
    middles = emit_mid.shape[0]

    def kernel(grand_ref, mid_ref, e_ref, m_ref, stat_ref):
        for i in range(groups):
            top = jnp.max(grand_ref[i], axis=0, keepdims=True)
            e = jnp.exp(grand_ref[i] - top)
            e_ref[i] = e
            stat_ref[i : i + 1, :] = top
            stat_ref[groups + middles + i : groups + middles + i + 1, :] = jnp.sum(e, axis=0, keepdims=True)
        for i in range(middles):
            top = jnp.max(mid_ref[i], axis=0, keepdims=True)
            m_ref[i] = jnp.exp(mid_ref[i] - top)
            stat_ref[groups + i : groups + i + 1, :] = top

    return pl.pallas_call(
        kernel,
        out_shape=(
            jax.ShapeDtypeStruct(emit_grand.shape, jnp.float32),
            jax.ShapeDtypeStruct(emit_mid.shape, jnp.float32),
            jax.ShapeDtypeStruct((2 * groups + middles, values), jnp.float32),
        ),
        name="prepare",
    )(emit_grand, emit_mid)


def halves(v):
    high = v.astype(jnp.bfloat16)
    return high, (v - high.astype(jnp.float32)).astype(jnp.bfloat16)


def edge_sums(w4, e, blocks):
    width, values = w4.shape[-1], e.shape[-1]
    count = len(blocks) // 2
    where = jnp.stack([jnp.stack([jnp.asarray(v, jnp.int32) for v in b]) for b in blocks])

    def kernel(where_ref, w_ref, e_ref, *out_refs):
        step = pl.program_id(0)
        wh, wl = halves(w_ref[0, 0, 0])
        eh, el = halves(e_ref[0])
        one = lambda p, q: jnp.dot(p, q, preferred_element_type=jnp.float32)
        got = one(wh, eh) + (one(wl, eh) + one(wh, el))
        for k in range(count):

            @pl.when(step // 2 == k)
            def _(k=k):
                out_refs[k][0] = got

    return pl.pallas_call(
        kernel,
        grid_spec=pltpu.PrefetchScalarGridSpec(
            num_scalar_prefetch=1,
            grid=(2 * count,),
            in_specs=[
                pl.BlockSpec((1, 1, 1, width, width), lambda s, w: (w[s, 0], w[s, 1], w[s, 2], 0, 0)),
                pl.BlockSpec((1, width, values), lambda s, w: (w[s, 0], 0, 0)),
            ],
            out_specs=[
                pl.BlockSpec((1, width, values), lambda s, w, k=k: (jnp.clip(s - 2 * k, 0, 1), 0, 0))
                for k in range(count)
            ],
        ),
        out_shape=[jax.ShapeDtypeStruct((2, width, values), jnp.float32)] * count,
        cost_estimate=pl.CostEstimate(
            flops=12 * count * width * width * values,
            bytes_accessed=16 * count * width * width,
            transcendentals=0,
        ),
        name="edge_sums",
    )(where, w4, e)


def hot(pixels, values):
    return (jnp.arange(values, dtype=jnp.int32)[:, None] == pixels[None, :]).astype(jnp.float32)


def dot(a, b, precision=HIGH):
    return jnp.dot(a, b, precision=precision)


def dot_t(a, b, precision=HIGH):
    return lax.dot_general(a, b, (((1,), (1,)), ((), ())), precision=precision)


def shards(
    pix_grand,
    pix_mid,
    pix_root,
    parent,
    emit_grand,
    emit_mid,
    emit_root,
    weight_grand,
    root_middle_weight,
    prior,
):
    f32 = jnp.float32
    images = pix_grand.shape[0]
    groups, states, width = weight_grand.shape
    middles, roots, _ = root_middle_weight.shape
    values = emit_root.shape[1]
    scale = states * states / images
    nodes = groups * lax.axis_size("leaf") + middles + 1
    place = lax.axis_index("panel")
    x, y = place // 4, place % 4

    def at(base, d):
        return (base + d + 4) % 4

    e_loc, mid_loc, stat = prepare(emit_grand, emit_mid)
    top_own = stat[: groups + middles]

    def merge(parts):
        top = parts[0][: groups + middles]
        for p in parts[1:]:
            top = jnp.maximum(top, p[: groups + middles])
        total = sum(
            p[groups + middles : 2 * groups + middles] * jnp.exp(p[:groups] - top[:groups]) for p in parts
        )
        return jnp.concatenate([top, total])

    from_x = {d: MOVE_X(stat, -d) for d in (1, -1, 2)}
    line = merge([stat, from_x[1], from_x[-1], from_x[2]])
    both = jnp.concatenate([line, stat])
    from_y = {d: MOVE_Y(both, -d) for d in (1, -1, 2)}
    stats = merge([line, from_y[1][:8], from_y[-1][:8], from_y[2][:8]])
    top_all = stats[: groups + middles]
    sum_all = stats[groups + middles :]
    shift_own = jnp.exp(top_own - top_all)
    shift_x = {0: shift_own[:groups]}
    shift_y = {0: shift_own[:groups]}
    for d in (1, -1):
        shift_x[d] = jnp.exp(from_x[d][:groups] - top_all[:groups])
        shift_y[d] = jnp.exp(from_y[d][8 : 8 + groups] - top_all[:groups])
    e_grand = e_loc * shift_own[:groups, None, :]
    e_mid_tab = mid_loc * shift_own[groups:, None, :]

    w4 = weight_grand.reshape(groups, 4, 4, width, width)
    e_loc, _ = lax.optimization_barrier((e_loc, both))

    def blocks(keys):
        out = []
        for g, d, h in keys:
            for r in (2 * h, 2 * h + 1):
                out.append((g, at(x, d), r) if g == 0 else (g, r, at(y, d)))
        return out

    far = [(0, 2, 0), (1, 2, 0), (0, 2, 1), (1, 2, 1)]
    raw = [(0, 1, 1), (1, 1, 1), (0, -1, 0), (1, -1, 0)]
    rest = [(g, d, h) for d, h in ((1, 0), (-1, 1), (0, 0), (0, 1)) for g in (0, 1)]
    made = dict(zip(far, edge_sums(w4, e_loc, blocks(far))))
    made.update(zip(raw, edge_sums(w4, e_loc, blocks(raw))))
    made.update(zip(rest, edge_sums(w4, e_grand, blocks(rest))))
    first_x = jnp.concatenate(
        ring_scatter(MOVE_X, lambda d, h, c=False: made[0, d, h], lambda v, d: v * shift_x[d][0], False)
    )
    first_y = jnp.concatenate(
        ring_scatter(MOVE_Y, lambda d, h, c=False: made[1, d, h], lambda v, d: v * shift_y[d][1], False)
    )

    def split(first, base):
        half = first.shape[1] // 2

        def piece(d, h):
            return lax.dynamic_slice(
                first, (at(base, d), half * h, 0), (1, half, first.shape[2])
            )[0]

        return piece

    s_own = jnp.stack(
        [
            jnp.concatenate(ring_scatter(MOVE_Y, split(first_x, y))),
            jnp.concatenate(ring_scatter(MOVE_X, split(first_y, x))),
        ]
    )
    norm = jnp.log(sum_all * MEAN_W)
    message = jnp.log(s_own) - norm[:, None, :]

    rows_of = images // values
    tail = [
        jnp.concatenate(
            [
                message[i],
                pix_grand[:, i].astype(f32).reshape(rows_of, values),
                jnp.broadcast_to(parent[i].astype(f32), (8 - rows_of, values)),
            ]
        )
        for i in range(groups)
    ]
    ring = ring_gather(MOVE_Z, *tail)
    near = {(d, 0): ring[d] for d in ring}
    for d in ring:
        got = lax.ppermute(jnp.stack(ring[d]), "leaf", hop_leaf(0, 1))
        near[d, 1] = (got[0], got[1])
    rel = [(d, flip) for d in (0, 1, -1, 2) for flip in (0, 1)]
    pix_of = {k: [near[k][i][width : width + rows_of].reshape(images).astype(jnp.int32) for i in range(groups)] for k in rel}
    parent_of = {k: [near[k][i][width + rows_of, 0].astype(jnp.int32) for i in range(groups)] for k in rel}
    child = [jnp.zeros((width, images), f32) for _ in range(middles)]
    for k in rel:
        for i in range(groups):
            got = dot(near[k][i][:width], hot(pix_of[k][i], values))
            for u in range(middles):
                child[u] = child[u] + jnp.where(parent_of[k][i] == u, got, 0.0)
    e_mid = [
        dot(e_mid_tab[u], hot(pix_mid[:, u], values)) * jnp.exp(child[u]) for u in range(middles)
    ]

    wm = root_middle_weight.reshape(middles, 4, 4, roots // 16, width)
    sub = roots // 16

    def mid_x(d, h):
        rows = lax.dynamic_slice(wm[h], (at(x, d), 0, 0, 0), (1, 4, sub, width)).reshape(4 * sub, width)
        return dot(rows, e_mid[h]).reshape(4, sub, images)

    def mid_y(d, h):
        rows = lax.dynamic_slice(wm[2 + h], (0, at(y, d), 0, 0), (4, 1, sub, width)).reshape(4 * sub, width)
        return dot(rows, e_mid[2 + h]).reshape(4, sub, images)

    line_x = ring_scatter(MOVE_X, mid_x)
    line_y = ring_scatter(MOVE_Y, mid_y)

    def pick(parts, base):
        return lambda d, h: lax.dynamic_slice(parts[h], (at(base, d), 0, 0), (1, sub, images))[0]

    own_x = ring_scatter(MOVE_Y, pick(line_x, y))
    own_y = ring_scatter(MOVE_X, pick(line_y, x))

    def order(blocks, base):
        out = jnp.stack([blocks[0], blocks[1], blocks[2], blocks[-1]])
        return jnp.roll(out, base, axis=0)

    def fill(first, first_base, second, second_base, parts, merged=True):
        got = ring_gather(first, *parts)
        rows = [order({d: got[d][h] for d in got}, first_base) for h in range(2)]
        got = ring_gather(second, *rows, merged)
        return [order({d: got[d][h] for d in got}, second_base) for h in range(2)]

    full_x = fill(MOVE_Y, y, MOVE_X, x, own_x)
    full_y = fill(MOVE_X, x, MOVE_Y, y, own_y)
    s_mid = [v.reshape(roots, images) for v in full_x] + [
        jnp.transpose(v, (1, 0, 2, 3)).reshape(roots, images) for v in full_y
    ]

    root_tab = prior[:, None] * jnp.exp(emit_root + LIFT)
    base = dot(root_tab, hot(pix_root, values))
    p01, p23 = s_mid[0] * s_mid[1], s_mid[2] * s_mid[3]
    t_mid = [base * s_mid[1] * p23, base * s_mid[0] * p23, base * p01 * s_mid[3], base * p01 * s_mid[2]]
    total_own = jnp.sum(base * p01 * p23, axis=0)
    level = top_all[:groups] + norm
    level_own = sum(dot(level, hot(pix_grand[:, i], values), HIGHEST)[i] for i in range(groups))
    tell = jnp.stack([total_own, level_own])
    tell = tell + lax.ppermute(tell, "leaf", hop_leaf(0, 1))
    tell = tell + MOVE_Z(tell, 1) + MOVE_Z(tell, -1) + MOVE_Z(tell, 2)
    total = tell[0]
    level_mid = sum(
        dot(top_all[groups:], hot(pix_mid[:, u], values), HIGHEST)[u] for u in range(middles)
    )
    loglik = (jnp.log(total) - LIFT + tell[1] + level_mid) / nodes

    part = 1.0 / total
    q_mid = [
        e_mid[u]
        * part
        * lax.dot_general(root_middle_weight[u], t_mid[u], (((0,), (0,)), ((), ())), precision=HIGH)
        for u in range(middles)
    ]
    flow_mid = jnp.stack(
        [
            root_middle_weight[u] * dot_t(t_mid[u], e_mid[u] * (part * scale))
            for u in range(middles)
        ]
    )

    def grouped(k, i):
        mine = sum(jnp.where(parent_of[k][i] == u, q_mid[u], 0.0) for u in range(middles))
        return dot_t(mine, hot(pix_of[k][i], values))

    q_own = {}
    for d in (2, 1, -1, 0):
        away = jnp.stack([grouped((d, 1), i) for i in range(groups)])
        here = jnp.stack([grouped((d, 0), i) for i in range(groups)])
        q_own[d] = here + lax.ppermute(away, "leaf", hop_leaf(0, 1))
    q_sum = ring_scatter(MOVE_Z, lambda d, h: q_own[d][h])
    ratio = [q_sum[i] / s_own[i] for i in range(groups)]

    half = width // 2
    t_x = fill(MOVE_Y, y, MOVE_X, x, (ratio[0][:half], ratio[0][half:]), False)
    t_y = fill(MOVE_X, x, MOVE_Y, y, (ratio[1][:half], ratio[1][half:]), False)
    t_0 = jnp.stack(t_x, axis=2).reshape(states, values)
    t_1 = jnp.transpose(jnp.stack(t_y, axis=2), (1, 0, 2, 3, 4)).reshape(states, values)
    flow_grand = jnp.stack(
        [
            weight_grand[0] * dot_t(t_0, e_grand[0] * scale),
            weight_grand[1] * dot_t(t_1, e_grand[1] * scale),
        ]
    )
    return (loglik, flow_grand, flow_mid)


def solution(mesh):
    placed = (
        P(None, "leaf"),
        P(),
        P(),
        P("leaf"),
        P("leaf", "panel", None),
        P(None, "panel", None),
        P("leaf", None),
        P("leaf", None, "panel"),
        P(None, "leaf", "panel"),
        P("leaf"),
    )
    return jax.shard_map(
        shards,
        mesh=mesh,
        in_specs=placed,
        out_specs=(P(), P("leaf", None, "panel"), P(None, "leaf", "panel")),
        check_vma=False,
    )
```

```python
import jax
import jax.numpy as jnp
from jax import lax
from jax.experimental import pallas as pl
from jax.experimental.pallas import tpu as pltpu
from jax.sharding import PartitionSpec as P


HIGH = lax.Precision.HIGH
HIGHEST = lax.Precision.HIGHEST
LIFT = 35.0
MEAN_W = 1.09e-4


def ring_x(d):
    return [(x * 4 + y, ((x + d) % 4) * 4 + y) for x in range(4) for y in range(4)]


def ring_y(d):
    return [(x * 4 + y, x * 4 + (y + d) % 4) for x in range(4) for y in range(4)]


def ring_z(d):
    return [(z * 2 + c, ((z + d) % 4) * 2 + c) for z in range(4) for c in range(2)]


def hop_leaf(d, flip):
    return [(z * 2 + c, ((z + d) % 4) * 2 + (c ^ flip)) for z in range(4) for c in range(2)]


def mover(axis, ring):
    return lambda v, d: lax.ppermute(v, axis, ring(d))


MOVE_X = mover("panel", ring_x)
MOVE_Y = mover("panel", ring_y)
MOVE_Z = mover("leaf", ring_z)


def ring_scatter(move, piece, scale=None, merged=True):
    if scale is None:
        scale = lambda v, d: v
        common = piece
    else:
        common = lambda d, h: piece(d, h, True)
    r1 = move(piece(2, 0), 1)
    r2 = move(piece(2, 1), -1)
    if merged:
        up = move(jnp.stack([common(1, 0) + scale(r1, -1), common(1, 1)]), 1)
        down = move(jnp.stack([common(-1, 0), common(-1, 1) + scale(r2, 1)]), -1)
        return common(0, 0) + up[0] + down[0], common(0, 1) + up[1] + down[1]
    r3 = move(piece(1, 1), 1)
    r4 = move(piece(-1, 0), -1)
    sums = common(1, 0) + scale(r1, -1), common(-1, 1) + scale(r2, 1)
    r5, r6 = move(sums[0], 1), move(sums[1], -1)
    return sums, lambda own0, own1: (own0 + scale(r4, 1) + r5, own1 + scale(r3, -1) + r6)


def ring_gather(move, half0, half1, merged=True):
    if merged:
        both = jnp.stack([half0, half1])
        a, b = move(both, 1), move(both, -1)
        return {0: (half0, half1), -1: (a[0], a[1]), 1: (b[0], b[1]), 2: (move(a[0], 1), move(b[1], -1))}
    a1 = move(half0, 1)
    b2 = move(half1, -1)
    b1 = move(half1, 1)
    a2 = move(half0, -1)
    a3 = move(a1, 1)
    b3 = move(b2, -1)
    return {0: (half0, half1), -1: (a1, b1), 1: (a2, b2), 2: (a3, b3)}


def scatter_direct(move, piece):
    return piece(0) + move(piece(1), 1) + move(piece(-1), -1) + move(piece(2), 2)


def gather_direct(move, block):
    return {0: block, -1: move(block, 1), 1: move(block, -1), 2: move(block, 2)}


def prepare(emit_grand, emit_mid):
    groups, width, values = emit_grand.shape
    middles = emit_mid.shape[0]

    def kernel(grand_ref, mid_ref, e_ref, e3_ref, m_ref, stat_ref):
        for i in range(groups):
            top = jnp.max(grand_ref[i], axis=0, keepdims=True)
            e = jnp.exp(grand_ref[i] - top)
            e_ref[i] = e
            put_triple(e3_ref, i, e)
            stat_ref[i : i + 1, :] = top
            stat_ref[groups + middles + i : groups + middles + i + 1, :] = jnp.sum(e, axis=0, keepdims=True)
        for i in range(middles):
            top = jnp.max(mid_ref[i], axis=0, keepdims=True)
            m_ref[i] = jnp.exp(mid_ref[i] - top)
            stat_ref[groups + i : groups + i + 1, :] = top

    return pl.pallas_call(
        kernel,
        out_shape=(
            jax.ShapeDtypeStruct(emit_grand.shape, jnp.float32),
            jax.ShapeDtypeStruct((groups, 3 * width, values), jnp.bfloat16),
            jax.ShapeDtypeStruct(emit_mid.shape, jnp.float32),
            jax.ShapeDtypeStruct((2 * groups + middles, values), jnp.float32),
        ),
        name="prepare",
    )(emit_grand, emit_mid)


def halves(v):
    high = v.astype(jnp.bfloat16)
    return high, (v - high.astype(jnp.float32)).astype(jnp.bfloat16)


def prepare(emit_grand, emit_mid):
    groups, width, values = emit_grand.shape
    middles = emit_mid.shape[0]

    def kernel(grand_ref, mid_ref, e_ref, e3_ref, m_ref, stat_ref):
        for i in range(groups):
            top = jnp.max(grand_ref[i], axis=0, keepdims=True)
            e = jnp.exp(grand_ref[i] - top)
            e_ref[i] = e
            put_triple(e3_ref, i, e)
            stat_ref[i : i + 1, :] = top
            stat_ref[groups + middles + i : groups + middles + i + 1, :] = jnp.sum(e, axis=0, keepdims=True)
        for i in range(middles):
            top = jnp.max(mid_ref[i], axis=0, keepdims=True)
            m_ref[i] = jnp.exp(mid_ref[i] - top)
            stat_ref[groups + i : groups + i + 1, :] = top

    return pl.pallas_call(
        kernel,
        out_shape=(
            jax.ShapeDtypeStruct(emit_grand.shape, jnp.float32),
            jax.ShapeDtypeStruct((groups, 3 * width, values), jnp.bfloat16),
            jax.ShapeDtypeStruct(emit_mid.shape, jnp.float32),
            jax.ShapeDtypeStruct((2 * groups + middles, values), jnp.float32),
        ),
        name="prepare",
    )(emit_grand, emit_mid)


def put_triple(ref, i, b):
    high, low = halves(b)
    rows = b.shape[0]
    ref[i, :rows] = high
    ref[i, rows : 2 * rows] = high
    ref[i, 2 * rows :] = low


def deep(a, b3):
    high, low = halves(a)
    return jnp.dot(jnp.concatenate([high, low, high], axis=1), b3, preferred_element_type=jnp.float32)


def rescale(e, shift, scale):
    groups, width, values = e.shape

    def kernel(e_ref, shift_ref, up_ref, down_ref):
        for i in range(groups):
            moved = e_ref[i] * shift_ref[i : i + 1, :]
            put_triple(up_ref, i, moved)
            put_triple(down_ref, i, jnp.transpose(moved * scale))

    return pl.pallas_call(
        kernel,
        out_shape=(
            jax.ShapeDtypeStruct((groups, 3 * width, values), jnp.bfloat16),
            jax.ShapeDtypeStruct((groups, 3 * values, width), jnp.bfloat16),
        ),
        name="rescale",
    )(e, shift)


def block_of(ref, spot_ref, group, d, h):
    line = lax.rem(spot_ref[group] + (d + 4), 4)
    if group == 0:
        return ref.at[0, line, pl.ds(2 * h, 2)]
    return ref.at[1, pl.ds(2 * h, 2), line]


ANY = pl.BlockSpec(memory_space=pl.ANY)


def edge_sums(spot, w4, e3, pieces, deps=()):
    width, values = w4.shape[-1], e3.shape[-1]
    count, waits = len(pieces), len(deps)

    def kernel(spot_ref, w_ref, e_ref, *refs):
        out_refs = refs[waits : waits + count]
        w_buf, out_buf, in_sem, out_sem = refs[waits + count :]
        ins, outs = [], []
        for k, (group, d, h) in enumerate(pieces):
            ins.append(pltpu.make_async_copy(block_of(w_ref, spot_ref, group, d, h), w_buf.at[k], in_sem.at[k]))
            ins[-1].start()
        for k, (group, _, _) in enumerate(pieces):
            ins[k].wait()
            got = deep(w_buf[k].reshape(2 * width, width), e_ref[group])
            out_buf[k] = got.reshape(2, width, values)
            outs.append(pltpu.make_async_copy(out_buf.at[k], out_refs[k], out_sem.at[k]))
            outs[-1].start()
        for copy in outs:
            copy.wait()

    return pl.pallas_call(
        kernel,
        in_specs=[pl.BlockSpec(memory_space=pltpu.SMEM), ANY, pl.BlockSpec(memory_space=pltpu.VMEM)] + [ANY] * waits,
        out_specs=[ANY] * count,
        out_shape=[jax.ShapeDtypeStruct((2, width, values), jnp.float32)] * count,
        scratch_shapes=[
            pltpu.VMEM((count, 2, width, width), jnp.float32),
            pltpu.VMEM((count, 2, width, values), jnp.float32),
            pltpu.SemaphoreType.DMA((count,)),
            pltpu.SemaphoreType.DMA((count,)),
        ],
        cost_estimate=pl.CostEstimate(
            flops=12 * count * width * width * values,
            bytes_accessed=16 * count * width * width,
            transcendentals=0,
        ),
        name="edge_sums",
    )(spot, w4, e3, *deps)


def children(blocks, width, images, middles, before=None, base=None, lines=()):
    values = blocks[0].shape[-1]
    lead = [] if before is None else list(before)
    lines = list(lines)
    last = [] if base is None else list(base)

    def kernel(*refs):
        block_refs = refs[: len(blocks)]
        lead_refs = refs[len(blocks) : len(blocks) + len(lead)]
        last_refs = refs[len(blocks) + len(lead) : len(blocks) + len(lead) + len(last)]
        ends = len(blocks) + len(lead) + len(last)
        line_refs = refs[ends : ends + len(lines)]
        out_refs, note_ref = refs[ends + len(lines) :][:middles], refs[ends + len(lines) + middles]
        sum_refs = refs[ends + len(lines) + middles + 1 :]
        spot = 0
        for u in range(middles):
            out_refs[u][...] = lead_refs[u][...] if lead else jnp.zeros((width, images), jnp.float32)
        for ref in block_refs:
            for i in range(ref.shape[0]):
                note = ref[i, width:, :]
                ids = lax.broadcasted_iota(jnp.int32, (values, values), 0).astype(jnp.float32)
                parts = images // values
                mark = jnp.concatenate(
                    [(ids == note[r : r + 1, :]).astype(jnp.bfloat16) for r in range(parts)], axis=1
                )
                note_ref[spot, 0:1, :] = jnp.concatenate([note[r : r + 1, :] for r in range(parts)], axis=1)
                note_ref[spot, 1:2, :] = jnp.concatenate([note[parts : parts + 1, :]] * parts, axis=1)
                spot += 1
                high, low = halves(ref[i, :width, :])
                got = jnp.dot(
                    jnp.concatenate([high, low], axis=1),
                    jnp.concatenate([mark, mark], axis=0),
                    preferred_element_type=jnp.float32,
                )
                owner = note[images // values : images // values + 1, :1]
                for u in range(middles):
                    out_refs[u][...] += jnp.where(owner == u, got, 0.0)
        if last:
            for u in range(middles):
                done = last_refs[u][...] * jnp.exp(out_refs[u][...])
                out_refs[u][...] = done
                if lines:
                    high, low = halves(done)
                    sum_refs[u][...] = deep(line_refs[u][...], jnp.concatenate([high, high, low], axis=0))

    return pl.pallas_call(
        kernel,
        out_shape=[jax.ShapeDtypeStruct((width, images), jnp.float32)] * middles
        + [jax.ShapeDtypeStruct((sum(b.shape[0] for b in blocks), 8, images), jnp.float32)]
        + [jax.ShapeDtypeStruct((v.shape[0], images), jnp.float32) for v in lines],
        cost_estimate=pl.CostEstimate(
            flops=4 * sum(b.shape[0] for b in blocks) * width * values * images,
            bytes_accessed=4 * (sum(b.size for b in blocks) + middles * width * images * (1 + bool(lead) + bool(last))),
            transcendentals=0,
        ),
        name="children",
    )(*blocks, *lead, *last, *lines)


def edge_flows(spot, w4, ratios, e3, group, before=None):
    width, values = w4.shape[-1], e3.shape[1] // 3
    keys = list(ratios)
    count = len(keys)
    extra = [] if before is None else [before]

    def kernel(spot_ref, w_ref, e_ref, *refs):
        ratio_refs = refs[:count]
        out_ref, w_buf, ratio_buf, out_buf, w_sem, ratio_sem, out_sem = refs[count + len(extra) :]
        ins, outs = [], []
        for k, (d, h) in enumerate(keys):
            one = pltpu.make_async_copy(ratio_refs[k], ratio_buf.at[k], ratio_sem.at[k])
            two = pltpu.make_async_copy(block_of(w_ref, spot_ref, group, d, h), w_buf.at[k], w_sem.at[k])
            one.start()
            two.start()
            ins.append((one, two))
        for k, (d, h) in enumerate(keys):
            ins[k][0].wait()
            got = deep(ratio_buf[k].reshape(2 * width, values), e_ref[group])
            ins[k][1].wait()
            out_buf[k] = w_buf[k] * got.reshape(2, width, width)
            outs.append(pltpu.make_async_copy(out_buf.at[k], block_of(out_ref, spot_ref, group, d, h), out_sem.at[k]))
            outs[-1].start()
        for copy in outs:
            copy.wait()

    return pl.pallas_call(
        kernel,
        in_specs=[pl.BlockSpec(memory_space=pltpu.SMEM), ANY, pl.BlockSpec(memory_space=pltpu.VMEM)]
        + [ANY] * (count + len(extra)),
        out_specs=ANY,
        out_shape=jax.ShapeDtypeStruct(w4.shape, jnp.float32),
        scratch_shapes=[
            pltpu.VMEM((count, 2, width, width), jnp.float32),
            pltpu.VMEM((count, 2, width, values), jnp.float32),
            pltpu.VMEM((count, 2, width, width), jnp.float32),
            pltpu.SemaphoreType.DMA((count,)),
            pltpu.SemaphoreType.DMA((count,)),
            pltpu.SemaphoreType.DMA((count,)),
        ],
        input_output_aliases={3 + count: 0} if extra else {},
        cost_estimate=pl.CostEstimate(
            flops=12 * count * width * width * values,
            bytes_accessed=24 * count * width * width,
            transcendentals=0,
        ),
        name="edge_flows",
    )(spot, w4, e3, *[ratios[k] for k in keys], *extra)


def after(v, array):
    return v + (0.0 * array[(0,) * array.ndim]).astype(v.dtype)


def hot(pixels, values):
    return (jnp.arange(values, dtype=jnp.int32)[:, None] == pixels[None, :]).astype(jnp.float32)


def dot(a, b, precision=HIGH):
    return jnp.dot(a, b, precision=precision)


def dot_t(a, b, precision=HIGH):
    return lax.dot_general(a, b, (((1,), (1,)), ((), ())), precision=precision)


def shards(
    pix_grand,
    pix_mid,
    pix_root,
    parent,
    emit_grand,
    emit_mid,
    emit_root,
    weight_grand,
    root_middle_weight,
    prior,
):
    f32 = jnp.float32
    images = pix_grand.shape[0]
    groups, states, width = weight_grand.shape
    middles, roots, _ = root_middle_weight.shape
    values = emit_root.shape[1]
    scale = states * states / images
    nodes = groups * lax.axis_size("leaf") + middles + 1
    place = lax.axis_index("panel")
    x, y = place // 4, place % 4

    def at(base, d):
        return (base + d + 4) % 4

    e_loc, e_loc3, mid_loc, stat = prepare(emit_grand, emit_mid)
    top_own = stat[: groups + middles]

    across = lax.axis_size("panel")
    every = lax.all_to_all(
        jnp.broadcast_to(stat[None], (across, *stat.shape)).reshape(-1, values), "panel", 0, 0, tiled=True
    ).reshape(across, *stat.shape)
    tops = every[:, : groups + middles]
    top_all = jnp.max(tops, axis=0)
    shifts = jnp.exp(tops - top_all[None])
    sum_all = jnp.sum(every[:, groups + middles :] * shifts[:, :groups], axis=0)

    def shift(px, py):
        return lax.dynamic_slice(shifts, (px * 4 + py, 0, 0), (1, groups + middles, values))[0]

    shift_own = shift(x, y)
    shift_x = {d: shift(at(x, d), y)[:groups] for d in (1, -1)}
    shift_y = {d: shift(x, at(y, d))[:groups] for d in (1, -1)}
    e_all3, e_out3 = rescale(e_loc, shift_own[:groups], scale)
    spot = jnp.stack([x, y]).astype(jnp.int32)
    e_mid_tab = mid_loc * shift_own[groups:, None, :]

    w4 = weight_grand.reshape(groups, 4, 4, width, width)

    far = [(0, 2, 0), (1, 2, 0), (0, 2, 1), (1, 2, 1)]
    raw = [(0, 1, 1), (1, 1, 1), (0, -1, 0), (1, -1, 0)]
    passed = [(0, 1, 0), (1, 1, 0), (0, -1, 1), (1, -1, 1)]
    own = [(0, 0, 0), (0, 0, 1), (1, 0, 0), (1, 0, 1)]
    made = dict(zip(far, edge_sums(spot, w4, e_loc3, far)))
    made.update(zip(raw, edge_sums(spot, w4, e_loc3, raw, (made[far[0]],))))
    made.update(zip(passed, edge_sums(spot, w4, e_all3, passed, (made[raw[0]],))))
    sums_x, close_x = ring_scatter(
        MOVE_X, lambda d, h, c=False: made[0, d, h], lambda v, d: v * shift_x[d][0], False
    )
    sums_y, close_y = ring_scatter(
        MOVE_Y, lambda d, h, c=False: made[1, d, h], lambda v, d: v * shift_y[d][1], False
    )
    made.update(zip(own, edge_sums(spot, w4, e_all3, own, (*sums_x, *sums_y))))
    first_x = jnp.concatenate(close_x(made[own[0]], made[own[1]]))
    first_y = jnp.concatenate(close_y(made[own[2]], made[own[3]]))

    def split(first, base):
        return lambda d: lax.dynamic_slice(first, (at(base, d), 0, 0), (1, *first.shape[1:]))[0]

    s_own = jnp.stack([scatter_direct(MOVE_Y, split(first_x, y)), scatter_direct(MOVE_X, split(first_y, x))])
    norm = jnp.log(sum_all * MEAN_W)
    message = jnp.log(s_own) - norm[:, None, :]

    rows_of = images // values
    pix_late, parent_late = after(pix_grand, first_x), after(parent, first_x)
    tail = [
        jnp.concatenate(
            [
                message[i],
                pix_late[:, i].astype(f32).reshape(rows_of, values),
                jnp.broadcast_to(parent_late[i].astype(f32), (8 - rows_of, values)),
            ]
        )
        for i in range(groups)
    ]
    mine = jnp.stack(tail)
    below, above = MOVE_Z(mine, 1), MOVE_Z(mine, -1)
    swap = lambda v: lax.ppermute(v, "leaf", hop_leaf(0, 1))
    opposite = jnp.stack([MOVE_Z(below[0], 1), MOVE_Z(above[1], -1)])
    near = {(0, 0): mine, (-1, 0): below, (1, 0): above, (2, 0): opposite}
    for d in (0, -1, 1, 2):
        near[d, 1] = swap(near[d, 0])
    mid_tab = after(e_mid_tab, first_x)
    base_mid = [dot(mid_tab[u], hot(after(pix_mid, first_x)[:, u], values)) for u in range(middles)]
    wm = root_middle_weight.reshape(middles, 4, 4, roots // 16, width)
    sub = roots // 16

    lines = {}
    x_late, y_late = after(x, first_x), after(y, first_y)
    for h in range(2):
        for d in (0, 1, -1, 2):
            lines[0, d, h] = lax.dynamic_slice(wm[h], (at(x_late, d), 0, 0, 0), (1, 4, sub, width)).reshape(4 * sub, width)
            lines[1, d, h] = lax.dynamic_slice(wm[2 + h], (0, at(y_late, d), 0, 0), (4, 1, sub, width)).reshape(4 * sub, width)
    lines = lax.optimization_barrier(lines)

    stages = [[(0, 0), (0, 1)], [(-1, 0), (1, 0), (-1, 1), (1, 1)], [(2, 0), (2, 1)]]
    notes_of_keys = []
    sums = None
    for keys in stages:
        last = keys is stages[-1]
        got = children(
            [near[k] for k in keys],
            width,
            images,
            middles,
            before=sums,
            base=base_mid if last else None,
            lines=[lines[g, 2, h] for g in range(2) for h in range(2)] if last else (),
        )
        sums, notes, far_sums = got[:middles], got[middles], got[middles + 1 :]
        notes_of_keys.append((keys, notes))
    e_mid = sums

    def mid_x(d, h):
        got = far_sums[h] if d == 2 else dot(lines[0, d, h], e_mid[h])
        return got.reshape(4, sub, images)

    def mid_y(d, h):
        got = far_sums[2 + h] if d == 2 else dot(lines[1, d, h], e_mid[2 + h])
        return got.reshape(4, sub, images)

    line_x = ring_scatter(MOVE_X, mid_x)
    line_y = ring_scatter(MOVE_Y, mid_y)

    note_of = {}
    for keys, notes in notes_of_keys:
        notes = after(notes, line_x[0])
        for j, k in enumerate(keys):
            note_of[k] = [notes[groups * j + i] for i in range(groups)]
    zero = after(jnp.int32(0), line_x[0])
    wm_late = [lax.dynamic_index_in_dim(root_middle_weight, zero + u, keepdims=False) for u in range(middles)]

    def pick(parts, base):
        return lambda d: jnp.stack(
            [lax.dynamic_slice(p, (at(base, d), 0, 0), (1, sub, images))[0] for p in parts]
        )

    own_x = scatter_direct(MOVE_Y, pick(line_x, y))
    own_y = scatter_direct(MOVE_X, pick(line_y, x))

    def order(blocks, base):
        out = jnp.stack([blocks[0], blocks[1], blocks[2], blocks[-1]])
        return jnp.roll(out, base, axis=0)

    def fill(first, first_base, second, second_base, block):
        got = gather_direct(first, block)
        rows = [order({d: got[d][h] for d in got}, first_base) for h in range(2)]
        got = ring_gather(second, *rows)
        return [order({d: got[d][h] for d in got}, second_base) for h in range(2)]

    full_x = fill(MOVE_Y, y, MOVE_X, x, own_x)
    full_y = fill(MOVE_X, x, MOVE_Y, y, own_y)
    s_mid = [v.reshape(roots, images) for v in full_x] + [
        jnp.transpose(v, (1, 0, 2, 3)).reshape(roots, images) for v in full_y
    ]

    root_tab = prior[:, None] * jnp.exp(after(emit_root, line_x[0]) + LIFT)
    base = lax.optimization_barrier(dot(root_tab, hot(pix_root, values)))
    p01, p23 = s_mid[0] * s_mid[1], s_mid[2] * s_mid[3]
    t_mid = [base * s_mid[1] * p23, base * s_mid[0] * p23, base * p01 * s_mid[3], base * p01 * s_mid[2]]
    total_own = jnp.sum(base * p01 * p23, axis=0)
    level = after(top_all[:groups] + norm, line_x[0])
    level_own = sum(dot(level, hot(pix_grand[:, i], values), HIGHEST)[i] for i in range(groups))
    tell = jnp.stack([total_own, level_own])
    leaves = lax.axis_size("leaf")
    tell = jnp.sum(
        lax.all_to_all(
            jnp.broadcast_to(tell[None], (leaves, 2, images)).reshape(leaves * 2, images), "leaf", 0, 0, tiled=True
        ).reshape(leaves, 2, images),
        axis=0,
    )
    total = tell[0]
    level_mid = sum(
        dot(after(top_all[groups:], line_x[0]), hot(pix_mid[:, u], values), HIGHEST)[u] for u in range(middles)
    )
    loglik = (jnp.log(total) - LIFT + tell[1] + level_mid) / nodes

    part = 1.0 / total
    q_mid = [
        e_mid[u]
        * part
        * lax.dot_general(wm_late[u], t_mid[u], (((0,), (0,)), ((), ())), precision=HIGH)
        for u in range(middles)
    ]
    flow_mid = jnp.stack(
        [
            wm_late[u] * dot_t(t_mid[u], e_mid[u] * (part * scale))
            for u in range(middles)
        ]
    )

    def grouped(k, i):
        note = note_of[k][i]
        mine = sum(jnp.where(note[1:2] == u, q_mid[u], 0.0) for u in range(middles))
        mark = jnp.arange(values, dtype=jnp.int32).astype(f32)[:, None] == note[0:1]
        return dot_t(mine, mark.astype(f32))

    q_own = {}
    for d in (2, 1, -1, 0):
        away = jnp.stack([grouped((d, 1), i) for i in range(groups)])
        here = jnp.stack([grouped((d, 0), i) for i in range(groups)])
        q_own[d] = here + lax.ppermute(away, "leaf", hop_leaf(0, 1))
    q_sum = ring_scatter(MOVE_Z, lambda d, h: q_own[d][h])
    ratio = [q_sum[i] / s_own[i] for i in range(groups)]


    def ratios(first, first_base, second, block):
        rows = order(gather_direct(first, block), first_base)
        got = ring_gather(second, rows[:2], rows[2:], False)
        return {(d, h): got[d][h] for d in got for h in range(2)}

    r_x = ratios(MOVE_Y, y, MOVE_X, ratio[0])
    r_y = ratios(MOVE_X, x, MOVE_Y, ratio[1])
    flow = None
    for steps in ((0,), (1, -1), (2,)):
        keys = [(d, h) for d in steps for h in range(2)]
        for group, held in ((0, r_x), (1, r_y)):
            flow = edge_flows(spot, w4, {k: held[k] for k in keys}, e_out3, group, flow)
    flow_grand = flow.reshape(groups, states, width)
    return (loglik, flow_grand, flow_mid)


def solution(mesh):
    placed = (
        P(None, "leaf"),
        P(),
        P(),
        P("leaf"),
        P("leaf", "panel", None),
        P(None, "panel", None),
        P("leaf", None),
        P("leaf", None, "panel"),
        P(None, "leaf", "panel"),
        P("leaf"),
    )
    return jax.shard_map(
        shards,
        mesh=mesh,
        in_specs=placed,
        out_specs=(P(), P("leaf", None, "panel"), P(None, "leaf", "panel")),
        check_vma=False,
    )
```

```python
import jax
import jax.numpy as jnp
from jax import lax
from jax.experimental import pallas as pl
from jax.experimental.pallas import tpu as pltpu
from jax.sharding import PartitionSpec as P


HIGH = lax.Precision.HIGH
HIGHEST = lax.Precision.HIGHEST
LIFT = 35.0
MEAN_W = 1.09e-4


def ring_x(d):
    return [(x * 4 + y, ((x + d) % 4) * 4 + y) for x in range(4) for y in range(4)]


def ring_y(d):
    return [(x * 4 + y, x * 4 + (y + d) % 4) for x in range(4) for y in range(4)]


def ring_z(d):
    return [(z * 2 + c, ((z + d) % 4) * 2 + c) for z in range(4) for c in range(2)]


def hop_leaf(d, flip):
    return [(z * 2 + c, ((z + d) % 4) * 2 + (c ^ flip)) for z in range(4) for c in range(2)]


def mover(axis, ring):
    return lambda v, d: lax.ppermute(v, axis, ring(d))


MOVE_X = mover("panel", ring_x)
MOVE_Y = mover("panel", ring_y)
MOVE_Z = mover("leaf", ring_z)


def ring_scatter(move, piece, scale=None, merged=True):
    if scale is None:
        scale = lambda v, d: v
        common = piece
    else:
        common = lambda d, h: piece(d, h, True)
    r1 = move(piece(2, 0), 1)
    r2 = move(piece(2, 1), -1)
    if merged:
        up = move(jnp.stack([common(1, 0) + scale(r1, -1), common(1, 1)]), 1)
        down = move(jnp.stack([common(-1, 0), common(-1, 1) + scale(r2, 1)]), -1)
        return common(0, 0) + up[0] + down[0], common(0, 1) + up[1] + down[1]
    r3 = move(piece(1, 1), 1)
    r4 = move(piece(-1, 0), -1)
    sums = common(1, 0) + scale(r1, -1), common(-1, 1) + scale(r2, 1)
    r5, r6 = move(sums[0], 1), move(sums[1], -1)
    return sums, lambda own0, own1: (own0 + scale(r4, 1) + r5, own1 + scale(r3, -1) + r6)


def ring_gather(move, half0, half1, merged=True):
    if merged:
        both = jnp.stack([half0, half1])
        a, b = move(both, 1), move(both, -1)
        return {0: (half0, half1), -1: (a[0], a[1]), 1: (b[0], b[1]), 2: (move(a[0], 1), move(b[1], -1))}
    a1 = move(half0, 1)
    b2 = move(half1, -1)
    b1 = move(half1, 1)
    a2 = move(half0, -1)
    a3 = move(a1, 1)
    b3 = move(b2, -1)
    return {0: (half0, half1), -1: (a1, b1), 1: (a2, b2), 2: (a3, b3)}


def scatter_direct(move, piece):
    return piece(0) + move(piece(1), 1) + move(piece(-1), -1) + move(piece(2), 2)


def gather_direct(move, block):
    return {0: block, -1: move(block, 1), 1: move(block, -1), 2: move(block, 2)}


def prepare(emit_grand, emit_mid):
    groups, width, values = emit_grand.shape
    middles = emit_mid.shape[0]

    def kernel(grand_ref, mid_ref, e_ref, e3_ref, m_ref, stat_ref):
        for i in range(groups):
            top = jnp.max(grand_ref[i], axis=0, keepdims=True)
            e = jnp.exp(grand_ref[i] - top)
            e_ref[i] = e
            put_triple(e3_ref, i, e)
            stat_ref[i : i + 1, :] = top
            stat_ref[groups + middles + i : groups + middles + i + 1, :] = jnp.sum(e, axis=0, keepdims=True)
        for i in range(middles):
            top = jnp.max(mid_ref[i], axis=0, keepdims=True)
            m_ref[i] = jnp.exp(mid_ref[i] - top)
            stat_ref[groups + i : groups + i + 1, :] = top

    return pl.pallas_call(
        kernel,
        out_shape=(
            jax.ShapeDtypeStruct(emit_grand.shape, jnp.float32),
            jax.ShapeDtypeStruct((groups, 3 * width, values), jnp.bfloat16),
            jax.ShapeDtypeStruct(emit_mid.shape, jnp.float32),
            jax.ShapeDtypeStruct((2 * groups + middles, values), jnp.float32),
        ),
        name="prepare",
    )(emit_grand, emit_mid)


def halves(v):
    high = v.astype(jnp.bfloat16)
    return high, (v - high.astype(jnp.float32)).astype(jnp.bfloat16)


def prepare(emit_grand, emit_mid):
    groups, width, values = emit_grand.shape
    middles = emit_mid.shape[0]

    def kernel(grand_ref, mid_ref, e_ref, e3_ref, m_ref, stat_ref):
        for i in range(groups):
            top = jnp.max(grand_ref[i], axis=0, keepdims=True)
            e = jnp.exp(grand_ref[i] - top)
            e_ref[i] = e
            put_triple(e3_ref, i, e)
            stat_ref[i : i + 1, :] = top
            stat_ref[groups + middles + i : groups + middles + i + 1, :] = jnp.sum(e, axis=0, keepdims=True)
        for i in range(middles):
            top = jnp.max(mid_ref[i], axis=0, keepdims=True)
            m_ref[i] = jnp.exp(mid_ref[i] - top)
            stat_ref[groups + i : groups + i + 1, :] = top

    return pl.pallas_call(
        kernel,
        out_shape=(
            jax.ShapeDtypeStruct(emit_grand.shape, jnp.float32),
            jax.ShapeDtypeStruct((groups, 3 * width, values), jnp.bfloat16),
            jax.ShapeDtypeStruct(emit_mid.shape, jnp.float32),
            jax.ShapeDtypeStruct((2 * groups + middles, values), jnp.float32),
        ),
        name="prepare",
    )(emit_grand, emit_mid)


def put_triple(ref, i, b):
    high, low = halves(b)
    rows = b.shape[0]
    ref[i, :rows] = high
    ref[i, rows : 2 * rows] = high
    ref[i, 2 * rows :] = low


def deep(a, b3):
    high, low = halves(a)
    return jnp.dot(jnp.concatenate([high, low, high], axis=1), b3, preferred_element_type=jnp.float32)


def rescale(e, shift, scale):
    groups, width, values = e.shape

    def kernel(e_ref, shift_ref, up_ref, down_ref):
        for i in range(groups):
            moved = e_ref[i] * shift_ref[i : i + 1, :]
            put_triple(up_ref, i, moved)
            put_triple(down_ref, i, jnp.transpose(moved * scale))

    return pl.pallas_call(
        kernel,
        out_shape=(
            jax.ShapeDtypeStruct((groups, 3 * width, values), jnp.bfloat16),
            jax.ShapeDtypeStruct((groups, 3 * values, width), jnp.bfloat16),
        ),
        name="rescale",
    )(e, shift)


def block_of(ref, spot_ref, group, d, h):
    line = lax.rem(spot_ref[group] + (d + 4), 4)
    if group == 0:
        return ref.at[0, line, pl.ds(2 * h, 2)]
    return ref.at[1, pl.ds(2 * h, 2), line]


ANY = pl.BlockSpec(memory_space=pl.ANY)


def edge_sums(spot, w4, e3, pieces, deps=()):
    width, values = w4.shape[-1], e3.shape[-1]
    count, waits = len(pieces), len(deps)

    def kernel(spot_ref, w_ref, e_ref, *refs):
        out_refs = refs[waits : waits + count]
        w_buf, out_buf, in_sem, out_sem = refs[waits + count :]
        for k, (group, d, h) in enumerate(pieces):
            pltpu.make_async_copy(block_of(w_ref, spot_ref, group, d, h), w_buf.at[k], in_sem.at[k]).start()
        outs = [pltpu.make_async_copy(out_buf.at[k], out_refs[k], out_sem.at[k]) for k in range(count)]

        @pl.loop(0, count)
        def _(k):
            pltpu.make_async_copy(w_ref.at[0, 0, pl.ds(0, 2)], w_buf.at[k], in_sem.at[k]).wait()
            got = deep(w_buf[k].reshape(2 * width, width), e_ref[lax.rem(k, 2)])
            out_buf[k] = got.reshape(2, width, values)
            for j in range(count):
                pl.when(k == j)(outs[j].start)

        for copy in outs:
            copy.wait()

    return pl.pallas_call(
        kernel,
        in_specs=[pl.BlockSpec(memory_space=pltpu.SMEM), ANY, pl.BlockSpec(memory_space=pltpu.VMEM)] + [ANY] * waits,
        out_specs=[ANY] * count,
        out_shape=[jax.ShapeDtypeStruct((2, width, values), jnp.float32)] * count,
        scratch_shapes=[
            pltpu.VMEM((count, 2, width, width), jnp.float32),
            pltpu.VMEM((count, 2, width, values), jnp.float32),
            pltpu.SemaphoreType.DMA((count,)),
            pltpu.SemaphoreType.DMA((count,)),
        ],
        cost_estimate=pl.CostEstimate(
            flops=12 * count * width * width * values,
            bytes_accessed=16 * count * width * width,
            transcendentals=0,
        ),
        name="edge_sums",
    )(spot, w4, e3, *deps)


def children(blocks, width, images, middles, before=None, base=None, lines=()):
    each, _, values = blocks[0].shape
    lead = [] if before is None else list(before)
    lines = list(lines)
    last = [] if base is None else list(base)

    def kernel(*refs):
        block_refs = refs[: len(blocks)]
        lead_refs = refs[len(blocks) : len(blocks) + len(lead)]
        last_refs = refs[len(blocks) + len(lead) : len(blocks) + len(lead) + len(last)]
        ends = len(blocks) + len(lead) + len(last)
        line_refs = refs[ends : ends + len(lines)]
        out_refs, note_ref = refs[ends + len(lines) :][:middles], refs[ends + len(lines) + middles]
        sum_refs = refs[ends + len(lines) + middles + 1 :]
        held, sem = sum_refs[len(lines) :]
        sum_refs = sum_refs[: len(lines)]
        parts = images // values
        for k, ref in enumerate(block_refs):
            pltpu.make_async_copy(ref, held.at[pl.ds(each * k, each)], sem.at[k]).start()
        for u in range(middles):
            out_refs[u][...] = lead_refs[u][...] if lead else jnp.zeros((width, images), jnp.float32)

        @pl.loop(0, len(blocks))
        def _(k):
            pltpu.make_async_copy(block_refs[0], held.at[pl.ds(each * k, each)], sem.at[k]).wait()

            @pl.loop(0, each)
            def _(i):
                s = each * k + i
                note = held[s, width:, :]
                ids = lax.broadcasted_iota(jnp.int32, (values, values), 0).astype(jnp.float32)
                mark = jnp.concatenate(
                    [(ids == note[r : r + 1, :]).astype(jnp.bfloat16) for r in range(parts)], axis=1
                )
                note_ref[s, 0:1, :] = jnp.concatenate([note[r : r + 1, :] for r in range(parts)], axis=1)
                note_ref[s, 1:2, :] = jnp.concatenate([note[parts : parts + 1, :]] * parts, axis=1)
                high, low = halves(held[s, :width, :])
                got = jnp.dot(
                    jnp.concatenate([high, low], axis=1),
                    jnp.concatenate([mark, mark], axis=0),
                    preferred_element_type=jnp.float32,
                )
                owner = note[parts : parts + 1, :1]
                for u in range(middles):
                    out_refs[u][...] += jnp.where(owner == u, got, 0.0)

        if last:
            for u in range(middles):
                done = last_refs[u][...] * jnp.exp(out_refs[u][...])
                out_refs[u][...] = done
                if lines:
                    high, low = halves(done)
                    sum_refs[u][...] = deep(line_refs[u][...], jnp.concatenate([high, high, low], axis=0))

    return pl.pallas_call(
        kernel,
        in_specs=[ANY] * len(blocks)
        + [pl.BlockSpec(memory_space=pltpu.VMEM)] * (len(lead) + len(last) + len(lines)),
        scratch_shapes=[
            pltpu.VMEM((each * len(blocks), width + 8, values), jnp.float32),
            pltpu.SemaphoreType.DMA((len(blocks),)),
        ],
        out_shape=[jax.ShapeDtypeStruct((width, images), jnp.float32)] * middles
        + [jax.ShapeDtypeStruct((sum(b.shape[0] for b in blocks), 8, images), jnp.float32)]
        + [jax.ShapeDtypeStruct((v.shape[0], images), jnp.float32) for v in lines],
        cost_estimate=pl.CostEstimate(
            flops=4 * sum(b.shape[0] for b in blocks) * width * values * images,
            bytes_accessed=4 * (sum(b.size for b in blocks) + middles * width * images * (1 + bool(lead) + bool(last))),
            transcendentals=0,
        ),
        name="children",
    )(*blocks, *lead, *last, *lines)


def edge_flows(spot, w4, ratios, e3, group, before=None):
    width, values = w4.shape[-1], e3.shape[1] // 3
    keys = list(ratios)
    count = len(keys)
    extra = [] if before is None else [before]

    def kernel(spot_ref, w_ref, e_ref, *refs):
        ratio_refs = refs[:count]
        out_ref, w_buf, ratio_buf, out_buf, w_sem, ratio_sem, out_sem = refs[count + len(extra) :]
        for k, (d, h) in enumerate(keys):
            pltpu.make_async_copy(ratio_refs[k], ratio_buf.at[k], ratio_sem.at[k]).start()
            pltpu.make_async_copy(block_of(w_ref, spot_ref, group, d, h), w_buf.at[k], w_sem.at[k]).start()
        outs = [
            pltpu.make_async_copy(out_buf.at[k], block_of(out_ref, spot_ref, group, d, h), out_sem.at[k])
            for k, (d, h) in enumerate(keys)
        ]

        @pl.loop(0, count)
        def _(k):
            pltpu.make_async_copy(ratio_refs[0], ratio_buf.at[k], ratio_sem.at[k]).wait()
            got = deep(ratio_buf[k].reshape(2 * width, values), e_ref[group])
            pltpu.make_async_copy(w_ref.at[0, 0, pl.ds(0, 2)], w_buf.at[k], w_sem.at[k]).wait()
            out_buf[k] = w_buf[k] * got.reshape(2, width, width)
            for j in range(count):
                pl.when(k == j)(outs[j].start)

        for copy in outs:
            copy.wait()

    return pl.pallas_call(
        kernel,
        in_specs=[pl.BlockSpec(memory_space=pltpu.SMEM), ANY, pl.BlockSpec(memory_space=pltpu.VMEM)]
        + [ANY] * (count + len(extra)),
        out_specs=ANY,
        out_shape=jax.ShapeDtypeStruct(w4.shape, jnp.float32),
        scratch_shapes=[
            pltpu.VMEM((count, 2, width, width), jnp.float32),
            pltpu.VMEM((count, 2, width, values), jnp.float32),
            pltpu.VMEM((count, 2, width, width), jnp.float32),
            pltpu.SemaphoreType.DMA((count,)),
            pltpu.SemaphoreType.DMA((count,)),
            pltpu.SemaphoreType.DMA((count,)),
        ],
        input_output_aliases={3 + count: 0} if extra else {},
        cost_estimate=pl.CostEstimate(
            flops=12 * count * width * width * values,
            bytes_accessed=24 * count * width * width,
            transcendentals=0,
        ),
        name="edge_flows",
    )(spot, w4, e3, *[ratios[k] for k in keys], *extra)


def after(v, array):
    return v + (0.0 * array[(0,) * array.ndim]).astype(v.dtype)


def hot(pixels, values):
    return (jnp.arange(values, dtype=jnp.int32)[:, None] == pixels[None, :]).astype(jnp.float32)


def dot(a, b, precision=HIGH):
    return jnp.dot(a, b, precision=precision)


def dot_t(a, b, precision=HIGH):
    return lax.dot_general(a, b, (((1,), (1,)), ((), ())), precision=precision)


def shards(
    pix_grand,
    pix_mid,
    pix_root,
    parent,
    emit_grand,
    emit_mid,
    emit_root,
    weight_grand,
    root_middle_weight,
    prior,
):
    f32 = jnp.float32
    images = pix_grand.shape[0]
    groups, states, width = weight_grand.shape
    middles, roots, _ = root_middle_weight.shape
    values = emit_root.shape[1]
    scale = states * states / images
    nodes = groups * lax.axis_size("leaf") + middles + 1
    place = lax.axis_index("panel")
    x, y = place // 4, place % 4

    def at(base, d):
        return (base + d + 4) % 4

    e_loc, e_loc3, mid_loc, stat = prepare(emit_grand, emit_mid)
    top_own = stat[: groups + middles]

    across = lax.axis_size("panel")
    every = lax.all_to_all(
        jnp.broadcast_to(stat[None], (across, *stat.shape)).reshape(-1, values), "panel", 0, 0, tiled=True
    ).reshape(across, *stat.shape)
    tops = every[:, : groups + middles]
    top_all = jnp.max(tops, axis=0)
    shifts = jnp.exp(tops - top_all[None])
    sum_all = jnp.sum(every[:, groups + middles :] * shifts[:, :groups], axis=0)

    def shift(px, py):
        return lax.dynamic_slice(shifts, (px * 4 + py, 0, 0), (1, groups + middles, values))[0]

    shift_own = shift(x, y)
    shift_x = {d: shift(at(x, d), y)[:groups] for d in (1, -1)}
    shift_y = {d: shift(x, at(y, d))[:groups] for d in (1, -1)}
    e_all3, e_out3 = rescale(e_loc, shift_own[:groups], scale)
    spot = jnp.stack([x, y]).astype(jnp.int32)
    e_mid_tab = mid_loc * shift_own[groups:, None, :]

    w4 = weight_grand.reshape(groups, 4, 4, width, width)

    far = [(0, 2, 0), (1, 2, 0), (0, 2, 1), (1, 2, 1)]
    raw = [(0, 1, 1), (1, 1, 1), (0, -1, 0), (1, -1, 0)]
    passed = [(0, 1, 0), (1, 1, 0), (0, -1, 1), (1, -1, 1)]
    own = [(0, 0, 0), (1, 0, 0), (0, 0, 1), (1, 0, 1)]
    made = dict(zip(far, edge_sums(spot, w4, e_loc3, far)))
    made.update(zip(raw, edge_sums(spot, w4, e_loc3, raw, (made[far[0]],))))
    made.update(zip(passed, edge_sums(spot, w4, e_all3, passed, (made[raw[0]],))))
    sums_x, close_x = ring_scatter(
        MOVE_X, lambda d, h, c=False: made[0, d, h], lambda v, d: v * shift_x[d][0], False
    )
    sums_y, close_y = ring_scatter(
        MOVE_Y, lambda d, h, c=False: made[1, d, h], lambda v, d: v * shift_y[d][1], False
    )
    made.update(zip(own, edge_sums(spot, w4, e_all3, own, (*sums_x, *sums_y))))
    first_x = jnp.concatenate(close_x(made[own[0]], made[own[2]]))
    first_y = jnp.concatenate(close_y(made[own[1]], made[own[3]]))

    def split(first, base):
        return lambda d: lax.dynamic_slice(first, (at(base, d), 0, 0), (1, *first.shape[1:]))[0]

    s_own = jnp.stack([scatter_direct(MOVE_Y, split(first_x, y)), scatter_direct(MOVE_X, split(first_y, x))])
    norm = jnp.log(sum_all * MEAN_W)
    message = jnp.log(s_own) - norm[:, None, :]

    rows_of = images // values
    pix_late, parent_late = after(pix_grand, first_x), after(parent, first_x)
    tail = [
        jnp.concatenate(
            [
                message[i],
                pix_late[:, i].astype(f32).reshape(rows_of, values),
                jnp.broadcast_to(parent_late[i].astype(f32), (8 - rows_of, values)),
            ]
        )
        for i in range(groups)
    ]
    mine = jnp.stack(tail)
    below, above = MOVE_Z(mine, 1), MOVE_Z(mine, -1)
    swap = lambda v: lax.ppermute(v, "leaf", hop_leaf(0, 1))
    opposite = jnp.stack([MOVE_Z(below[0], 1), MOVE_Z(above[1], -1)])
    near = {(0, 0): mine, (-1, 0): below, (1, 0): above, (2, 0): opposite}
    for d in (0, -1, 1, 2):
        near[d, 1] = swap(near[d, 0])
    mid_tab = after(e_mid_tab, first_x)
    base_mid = [dot(mid_tab[u], hot(after(pix_mid, first_x)[:, u], values)) for u in range(middles)]
    wm = root_middle_weight.reshape(middles, 4, 4, roots // 16, width)
    sub = roots // 16

    lines = {}
    x_late, y_late = after(x, first_x), after(y, first_y)
    for h in range(2):
        for d in (0, 1, -1, 2):
            lines[0, d, h] = lax.dynamic_slice(wm[h], (at(x_late, d), 0, 0, 0), (1, 4, sub, width)).reshape(4 * sub, width)
            lines[1, d, h] = lax.dynamic_slice(wm[2 + h], (0, at(y_late, d), 0, 0), (4, 1, sub, width)).reshape(4 * sub, width)
    lines = lax.optimization_barrier(lines)

    stages = [[(0, 0), (0, 1)], [(-1, 0), (1, 0), (-1, 1), (1, 1)], [(2, 0), (2, 1)]]
    notes_of_keys = []
    sums = None
    for keys in stages:
        last = keys is stages[-1]
        got = children(
            [near[k] for k in keys],
            width,
            images,
            middles,
            before=sums,
            base=base_mid if last else None,
            lines=[lines[g, 2, h] for g in range(2) for h in range(2)] if last else (),
        )
        sums, notes, far_sums = got[:middles], got[middles], got[middles + 1 :]
        notes_of_keys.append((keys, notes))
    e_mid = sums

    def mid_x(d, h):
        got = far_sums[h] if d == 2 else dot(lines[0, d, h], e_mid[h])
        return got.reshape(4, sub, images)

    def mid_y(d, h):
        got = far_sums[2 + h] if d == 2 else dot(lines[1, d, h], e_mid[2 + h])
        return got.reshape(4, sub, images)

    line_x = ring_scatter(MOVE_X, mid_x)
    line_y = ring_scatter(MOVE_Y, mid_y)

    note_of = {}
    for keys, notes in notes_of_keys:
        notes = after(notes, line_x[0])
        for j, k in enumerate(keys):
            note_of[k] = [notes[groups * j + i] for i in range(groups)]
    zero = after(jnp.int32(0), line_x[0])
    wm_late = [lax.dynamic_index_in_dim(root_middle_weight, zero + u, keepdims=False) for u in range(middles)]

    def pick(parts, base):
        return lambda d: jnp.stack(
            [lax.dynamic_slice(p, (at(base, d), 0, 0), (1, sub, images))[0] for p in parts]
        )

    own_x = scatter_direct(MOVE_Y, pick(line_x, y))
    own_y = scatter_direct(MOVE_X, pick(line_y, x))

    def order(blocks, base):
        out = jnp.stack([blocks[0], blocks[1], blocks[2], blocks[-1]])
        return jnp.roll(out, base, axis=0)

    def fill(first, first_base, second, second_base, block):
        got = gather_direct(first, block)
        rows = [order({d: got[d][h] for d in got}, first_base) for h in range(2)]
        got = ring_gather(second, *rows)
        return [order({d: got[d][h] for d in got}, second_base) for h in range(2)]

    full_x = fill(MOVE_Y, y, MOVE_X, x, own_x)
    full_y = fill(MOVE_X, x, MOVE_Y, y, own_y)
    s_mid = [v.reshape(roots, images) for v in full_x] + [
        jnp.transpose(v, (1, 0, 2, 3)).reshape(roots, images) for v in full_y
    ]

    root_tab = prior[:, None] * jnp.exp(after(emit_root, line_x[0]) + LIFT)
    base = lax.optimization_barrier(dot(root_tab, hot(pix_root, values)))
    p01, p23 = s_mid[0] * s_mid[1], s_mid[2] * s_mid[3]
    t_mid = [base * s_mid[1] * p23, base * s_mid[0] * p23, base * p01 * s_mid[3], base * p01 * s_mid[2]]
    total_own = jnp.sum(base * p01 * p23, axis=0)
    level = after(top_all[:groups] + norm, line_x[0])
    level_own = sum(dot(level, hot(pix_grand[:, i], values), HIGHEST)[i] for i in range(groups))
    tell = jnp.stack([total_own, level_own])
    leaves = lax.axis_size("leaf")
    tell = jnp.sum(
        lax.all_to_all(
            jnp.broadcast_to(tell[None], (leaves, 2, images)).reshape(leaves * 2, images), "leaf", 0, 0, tiled=True
        ).reshape(leaves, 2, images),
        axis=0,
    )
    total = tell[0]
    level_mid = sum(
        dot(after(top_all[groups:], line_x[0]), hot(pix_mid[:, u], values), HIGHEST)[u] for u in range(middles)
    )
    loglik = (jnp.log(total) - LIFT + tell[1] + level_mid) / nodes

    part = 1.0 / total
    q_mid = [
        e_mid[u]
        * part
        * lax.dot_general(wm_late[u], t_mid[u], (((0,), (0,)), ((), ())), precision=HIGH)
        for u in range(middles)
    ]
    flow_mid = jnp.stack(
        [
            wm_late[u] * dot_t(t_mid[u], e_mid[u] * (part * scale))
            for u in range(middles)
        ]
    )

    def grouped(k, i):
        note = note_of[k][i]
        mine = sum(jnp.where(note[1:2] == u, q_mid[u], 0.0) for u in range(middles))
        mark = jnp.arange(values, dtype=jnp.int32).astype(f32)[:, None] == note[0:1]
        return dot_t(mine, mark.astype(f32))

    q_own = {}
    for d in (2, 1, -1, 0):
        away = jnp.stack([grouped((d, 1), i) for i in range(groups)])
        here = jnp.stack([grouped((d, 0), i) for i in range(groups)])
        q_own[d] = here + lax.ppermute(away, "leaf", hop_leaf(0, 1))
    q_sum = ring_scatter(MOVE_Z, lambda d, h: q_own[d][h])
    ratio = [q_sum[i] / s_own[i] for i in range(groups)]


    def ratios(first, first_base, second, block):
        rows = order(gather_direct(first, block), first_base)
        got = ring_gather(second, rows[:2], rows[2:], False)
        return {(d, h): got[d][h] for d in got for h in range(2)}

    r_x = ratios(MOVE_Y, y, MOVE_X, ratio[0])
    r_y = ratios(MOVE_X, x, MOVE_Y, ratio[1])
    flow = None
    for steps in ((0, 1, -1), (2,)):
        keys = [(d, h) for d in steps for h in range(2)]
        for group, held in ((0, r_x), (1, r_y)):
            flow = edge_flows(spot, w4, {k: held[k] for k in keys}, e_out3, group, flow)
    flow_grand = flow.reshape(groups, states, width)
    return (loglik, flow_grand, flow_mid)


def solution(mesh):
    placed = (
        P(None, "leaf"),
        P(),
        P(),
        P("leaf"),
        P("leaf", "panel", None),
        P(None, "panel", None),
        P("leaf", None),
        P("leaf", None, "panel"),
        P(None, "leaf", "panel"),
        P("leaf"),
    )
    return jax.shard_map(
        shards,
        mesh=mesh,
        in_specs=placed,
        out_specs=(P(), P("leaf", None, "panel"), P(None, "leaf", "panel")),
        check_vma=False,
    )
```

```python
import jax
import jax.numpy as jnp
from jax import lax
from jax.experimental import pallas as pl
from jax.experimental.pallas import tpu as pltpu
from jax.sharding import PartitionSpec as P


HIGH = lax.Precision.HIGH
HIGHEST = lax.Precision.HIGHEST
LIFT = 35.0
MEAN_W = 1.09e-4


def ring_x(d):
    return [(x * 4 + y, ((x + d) % 4) * 4 + y) for x in range(4) for y in range(4)]


def ring_y(d):
    return [(x * 4 + y, x * 4 + (y + d) % 4) for x in range(4) for y in range(4)]


def ring_z(d):
    return [(z * 2 + c, ((z + d) % 4) * 2 + c) for z in range(4) for c in range(2)]


def hop_leaf(d, flip):
    return [(z * 2 + c, ((z + d) % 4) * 2 + (c ^ flip)) for z in range(4) for c in range(2)]


def mover(axis, ring):
    return lambda v, d: lax.ppermute(v, axis, ring(d))


MOVE_X = mover("panel", ring_x)
MOVE_Y = mover("panel", ring_y)
MOVE_Z = mover("leaf", ring_z)


def ring_scatter(move, piece, scale=None, merged=True):
    if scale is None:
        scale = lambda v, d: v
        common = piece
    else:
        common = lambda d, h: piece(d, h, True)
    r1 = move(piece(2, 0), 1)
    r2 = move(piece(2, 1), -1)
    if merged:
        up = move(jnp.stack([common(1, 0) + scale(r1, -1), common(1, 1)]), 1)
        down = move(jnp.stack([common(-1, 0), common(-1, 1) + scale(r2, 1)]), -1)
        return common(0, 0) + up[0] + down[0], common(0, 1) + up[1] + down[1]
    r3 = move(piece(1, 1), 1)
    r4 = move(piece(-1, 0), -1)
    sums = common(1, 0) + scale(r1, -1), common(-1, 1) + scale(r2, 1)
    r5, r6 = move(sums[0], 1), move(sums[1], -1)
    return sums, lambda own0, own1: (own0 + scale(r4, 1) + r5, own1 + scale(r3, -1) + r6)


def ring_gather(move, half0, half1, merged=True):
    if merged:
        both = jnp.stack([half0, half1])
        a, b = move(both, 1), move(both, -1)
        return {0: (half0, half1), -1: (a[0], a[1]), 1: (b[0], b[1]), 2: (move(a[0], 1), move(b[1], -1))}
    a1 = move(half0, 1)
    b2 = move(half1, -1)
    b1 = move(half1, 1)
    a2 = move(half0, -1)
    a3 = move(a1, 1)
    b3 = move(b2, -1)
    return {0: (half0, half1), -1: (a1, b1), 1: (a2, b2), 2: (a3, b3)}


def scatter_direct(move, piece):
    return piece(0) + move(piece(1), 1) + move(piece(-1), -1) + move(piece(2), 2)


def gather_direct(move, block):
    return {0: block, -1: move(block, 1), 1: move(block, -1), 2: move(block, 2)}


def prepare(emit_grand, emit_mid):
    groups, width, values = emit_grand.shape
    middles = emit_mid.shape[0]

    def kernel(grand_ref, mid_ref, e_ref, e3_ref, m_ref, stat_ref):
        for i in range(groups):
            top = jnp.max(grand_ref[i], axis=0, keepdims=True)
            e = jnp.exp(grand_ref[i] - top)
            e_ref[i] = e
            put_triple(e3_ref, i, e)
            stat_ref[i : i + 1, :] = top
            stat_ref[groups + middles + i : groups + middles + i + 1, :] = jnp.sum(e, axis=0, keepdims=True)
        for i in range(middles):
            top = jnp.max(mid_ref[i], axis=0, keepdims=True)
            m_ref[i] = jnp.exp(mid_ref[i] - top)
            stat_ref[groups + i : groups + i + 1, :] = top

    return pl.pallas_call(
        kernel,
        out_shape=(
            jax.ShapeDtypeStruct(emit_grand.shape, jnp.float32),
            jax.ShapeDtypeStruct((groups, 3 * width, values), jnp.bfloat16),
            jax.ShapeDtypeStruct(emit_mid.shape, jnp.float32),
            jax.ShapeDtypeStruct((2 * groups + middles, values), jnp.float32),
        ),
        name="prepare",
    )(emit_grand, emit_mid)


def halves(v):
    high = v.astype(jnp.bfloat16)
    return high, (v - high.astype(jnp.float32)).astype(jnp.bfloat16)


def prepare(emit_grand, emit_mid):
    groups, width, values = emit_grand.shape
    middles = emit_mid.shape[0]

    def kernel(grand_ref, mid_ref, e_ref, e3_ref, m_ref, stat_ref):
        for i in range(groups):
            top = jnp.max(grand_ref[i], axis=0, keepdims=True)
            e = jnp.exp(grand_ref[i] - top)
            e_ref[i] = e
            put_triple(e3_ref, i, e)
            stat_ref[i : i + 1, :] = top
            stat_ref[groups + middles + i : groups + middles + i + 1, :] = jnp.sum(e, axis=0, keepdims=True)
        for i in range(middles):
            top = jnp.max(mid_ref[i], axis=0, keepdims=True)
            m_ref[i] = jnp.exp(mid_ref[i] - top)
            stat_ref[groups + i : groups + i + 1, :] = top

    return pl.pallas_call(
        kernel,
        out_shape=(
            jax.ShapeDtypeStruct(emit_grand.shape, jnp.float32),
            jax.ShapeDtypeStruct((groups, 3 * width, values), jnp.bfloat16),
            jax.ShapeDtypeStruct(emit_mid.shape, jnp.float32),
            jax.ShapeDtypeStruct((2 * groups + middles, values), jnp.float32),
        ),
        name="prepare",
    )(emit_grand, emit_mid)


def put_triple(ref, i, b):
    high, low = halves(b)
    rows = b.shape[0]
    ref[i, :rows] = high
    ref[i, rows : 2 * rows] = high
    ref[i, 2 * rows :] = low


def deep(a, b3):
    high, low = halves(a)
    return jnp.dot(jnp.concatenate([high, low, high], axis=1), b3, preferred_element_type=jnp.float32)


def rescale(e, shift, scale):
    groups, width, values = e.shape

    def kernel(e_ref, shift_ref, up_ref, down_ref):
        for i in range(groups):
            moved = e_ref[i] * shift_ref[i : i + 1, :]
            put_triple(up_ref, i, moved)
            put_triple(down_ref, i, jnp.transpose(moved * scale))

    return pl.pallas_call(
        kernel,
        out_shape=(
            jax.ShapeDtypeStruct((groups, 3 * width, values), jnp.bfloat16),
            jax.ShapeDtypeStruct((groups, 3 * values, width), jnp.bfloat16),
        ),
        name="rescale",
    )(e, shift)


def block_of(ref, spot_ref, group, d, h):
    line = lax.rem(spot_ref[group] + (d + 4), 4)
    if group == 0:
        return ref.at[0, line, pl.ds(2 * h, 2)]
    return ref.at[1, pl.ds(2 * h, 2), line]


ANY = pl.BlockSpec(memory_space=pl.ANY)


def edge_sums(spot, w4, e3, pieces, deps=(), addends=(), factors=None):
    width, values = w4.shape[-1], e3.shape[-1]
    count, waits, more = len(pieces), len(deps), len(addends)
    rows = [] if factors is None else [factors]

    def kernel(spot_ref, w_ref, e_ref, *refs):
        add_refs, refs = refs[waits : waits + more], refs[waits + more :]
        row_refs, refs = refs[: len(rows)], refs[len(rows) :]
        out_refs = refs[:count]
        w_buf, out_buf, in_sem, out_sem, *add = refs[count:]
        for k in range(more):
            pltpu.make_async_copy(add_refs[k], add[0].at[k], add[1].at[k]).start()
        for k, (group, d, h) in enumerate(pieces):
            pltpu.make_async_copy(block_of(w_ref, spot_ref, group, d, h), w_buf.at[k], in_sem.at[k]).start()
        outs = [pltpu.make_async_copy(out_buf.at[k], out_refs[k], out_sem.at[k]) for k in range(count)]

        @pl.loop(0, count)
        def _(k):
            pltpu.make_async_copy(w_ref.at[0, 0, pl.ds(0, 2)], w_buf.at[k], in_sem.at[k]).wait()
            got = deep(w_buf[k].reshape(2 * width, width), e_ref[lax.rem(k, 2)])
            got = got.reshape(2, width, values)
            if more:
                pltpu.make_async_copy(add_refs[0], add[0].at[k], add[1].at[k]).wait()
                got = got + add[0][k] * row_refs[0][k]
            out_buf[k] = got
            for j in range(count):
                pl.when(k == j)(outs[j].start)

        for copy in outs:
            copy.wait()

    return pl.pallas_call(
        kernel,
        in_specs=[pl.BlockSpec(memory_space=pltpu.SMEM), ANY, pl.BlockSpec(memory_space=pltpu.VMEM)]
        + [ANY] * (waits + more)
        + [pl.BlockSpec(memory_space=pltpu.VMEM)] * len(rows),
        out_specs=[ANY] * count,
        out_shape=[jax.ShapeDtypeStruct((2, width, values), jnp.float32)] * count,
        scratch_shapes=[
            pltpu.VMEM((count, 2, width, width), jnp.float32),
            pltpu.VMEM((count, 2, width, values), jnp.float32),
            pltpu.SemaphoreType.DMA((count,)),
            pltpu.SemaphoreType.DMA((count,)),
        ]
        + ([pltpu.VMEM((count, 2, width, values), jnp.float32), pltpu.SemaphoreType.DMA((count,))] if more else []),
        cost_estimate=pl.CostEstimate(
            flops=12 * count * width * width * values,
            bytes_accessed=16 * count * width * width,
            transcendentals=0,
        ),
        name="edge_sums",
    )(spot, w4, e3, *deps, *addends, *rows)


def children(blocks, width, images, middles, before=None, base=None, lines=(), tables=None, marks=None):
    values = blocks[0].shape[-1]
    lead = [] if before is None else list(before)
    lines = list(lines)
    looked = [] if tables is None else [tables, marks]
    last = [] if base is None else list(base)

    def kernel(*refs):
        block_refs = refs[: len(blocks)]
        lead_refs = refs[len(blocks) : len(blocks) + len(lead)]
        last_refs = refs[len(blocks) + len(lead) : len(blocks) + len(lead) + len(last)]
        ends = len(blocks) + len(lead) + len(last)
        line_refs = refs[ends : ends + len(lines)]
        ends += len(lines)
        look_refs = refs[ends : ends + len(looked)]
        ends += len(looked)
        out_refs, note_ref = refs[ends : ends + middles], refs[ends + middles]
        sum_refs = refs[ends + middles + 1 :]
        for u in range(middles if looked else 0):
            ids = lax.broadcasted_iota(jnp.int32, (values, images), 0).astype(jnp.float32)
            mark = (ids == look_refs[1][u : u + 1, :]).astype(jnp.bfloat16)
            high, low = halves(look_refs[0][u])
            sum_refs[u][...] = jnp.dot(
                jnp.concatenate([high, low], axis=1),
                jnp.concatenate([mark, mark], axis=0),
                preferred_element_type=jnp.float32,
            )
        spot = 0
        for u in range(middles):
            out_refs[u][...] = lead_refs[u][...] if lead else jnp.zeros((width, images), jnp.float32)
        for ref in block_refs:
            for i in range(ref.shape[0]):
                note = ref[i, width:, :]
                ids = lax.broadcasted_iota(jnp.int32, (values, values), 0).astype(jnp.float32)
                parts = images // values
                mark = jnp.concatenate(
                    [(ids == note[r : r + 1, :]).astype(jnp.bfloat16) for r in range(parts)], axis=1
                )
                note_ref[spot, 0:1, :] = jnp.concatenate([note[r : r + 1, :] for r in range(parts)], axis=1)
                note_ref[spot, 1:2, :] = jnp.concatenate([note[parts : parts + 1, :]] * parts, axis=1)
                spot += 1
                high, low = halves(ref[i, :width, :])
                got = jnp.dot(
                    jnp.concatenate([high, low], axis=1),
                    jnp.concatenate([mark, mark], axis=0),
                    preferred_element_type=jnp.float32,
                )
                owner = note[images // values : images // values + 1, :1]
                for u in range(middles):
                    out_refs[u][...] += jnp.where(owner == u, got, 0.0)
        if last:
            for u in range(middles):
                done = last_refs[u][...] * jnp.exp(out_refs[u][...])
                out_refs[u][...] = done
                if lines:
                    high, low = halves(done)
                    sum_refs[u][...] = deep(line_refs[u][...], jnp.concatenate([high, high, low], axis=0))

    return pl.pallas_call(
        kernel,
        out_shape=[jax.ShapeDtypeStruct((width, images), jnp.float32)] * middles
        + [jax.ShapeDtypeStruct((sum(b.shape[0] for b in blocks), 8, images), jnp.float32)]
        + [jax.ShapeDtypeStruct((v.shape[0], images), jnp.float32) for v in lines]
        + [jax.ShapeDtypeStruct((width, images), jnp.float32)] * (middles if looked else 0),
        cost_estimate=pl.CostEstimate(
            flops=4 * sum(b.shape[0] for b in blocks) * width * values * images,
            bytes_accessed=4 * (sum(b.size for b in blocks) + middles * width * images * (1 + bool(lead) + bool(last))),
            transcendentals=0,
        ),
        name="children",
    )(*blocks, *lead, *last, *lines, *looked)


def edge_flows(spot, w4, ratios, e3, group, before=None):
    width, values = w4.shape[-1], e3.shape[1] // 3
    keys = list(ratios)
    count = len(keys)
    extra = [] if before is None else [before]

    def kernel(spot_ref, w_ref, e_ref, *refs):
        ratio_refs = refs[:count]
        out_ref, w_buf, ratio_buf, out_buf, w_sem, ratio_sem, out_sem = refs[count + len(extra) :]
        for k, (d, h) in enumerate(keys):
            pltpu.make_async_copy(ratio_refs[k], ratio_buf.at[k], ratio_sem.at[k]).start()
            pltpu.make_async_copy(block_of(w_ref, spot_ref, group, d, h), w_buf.at[k], w_sem.at[k]).start()
        outs = [
            pltpu.make_async_copy(out_buf.at[k], block_of(out_ref, spot_ref, group, d, h), out_sem.at[k])
            for k, (d, h) in enumerate(keys)
        ]

        @pl.loop(0, count)
        def _(k):
            pltpu.make_async_copy(ratio_refs[0], ratio_buf.at[k], ratio_sem.at[k]).wait()
            got = deep(ratio_buf[k].reshape(2 * width, values), e_ref[group])
            pltpu.make_async_copy(w_ref.at[0, 0, pl.ds(0, 2)], w_buf.at[k], w_sem.at[k]).wait()
            out_buf[k] = w_buf[k] * got.reshape(2, width, width)
            for j in range(count):
                pl.when(k == j)(outs[j].start)

        for copy in outs:
            copy.wait()

    return pl.pallas_call(
        kernel,
        in_specs=[pl.BlockSpec(memory_space=pltpu.SMEM), ANY, pl.BlockSpec(memory_space=pltpu.VMEM)]
        + [ANY] * (count + len(extra)),
        out_specs=ANY,
        out_shape=jax.ShapeDtypeStruct(w4.shape, jnp.float32),
        scratch_shapes=[
            pltpu.VMEM((count, 2, width, width), jnp.float32),
            pltpu.VMEM((count, 2, width, values), jnp.float32),
            pltpu.VMEM((count, 2, width, width), jnp.float32),
            pltpu.SemaphoreType.DMA((count,)),
            pltpu.SemaphoreType.DMA((count,)),
            pltpu.SemaphoreType.DMA((count,)),
        ],
        input_output_aliases={3 + count: 0} if extra else {},
        cost_estimate=pl.CostEstimate(
            flops=12 * count * width * width * values,
            bytes_accessed=24 * count * width * width,
            transcendentals=0,
        ),
        name="edge_flows",
    )(spot, w4, e3, *[ratios[k] for k in keys], *extra)


def after(v, array):
    return v + (0.0 * array[(0,) * array.ndim]).astype(v.dtype)


def hot(pixels, values):
    return (jnp.arange(values, dtype=jnp.int32)[:, None] == pixels[None, :]).astype(jnp.float32)


def dot(a, b, precision=HIGH):
    return jnp.dot(a, b, precision=precision)


def dot_t(a, b, precision=HIGH):
    return lax.dot_general(a, b, (((1,), (1,)), ((), ())), precision=precision)


def shards(
    pix_grand,
    pix_mid,
    pix_root,
    parent,
    emit_grand,
    emit_mid,
    emit_root,
    weight_grand,
    root_middle_weight,
    prior,
):
    f32 = jnp.float32
    images = pix_grand.shape[0]
    groups, states, width = weight_grand.shape
    middles, roots, _ = root_middle_weight.shape
    values = emit_root.shape[1]
    scale = states * states / images
    nodes = groups * lax.axis_size("leaf") + middles + 1
    place = lax.axis_index("panel")
    x, y = place // 4, place % 4

    def at(base, d):
        return (base + d + 4) % 4

    e_loc, e_loc3, mid_loc, stat = prepare(emit_grand, emit_mid)
    top_own = stat[: groups + middles]

    across = lax.axis_size("panel")
    every = lax.all_to_all(
        jnp.broadcast_to(stat[None], (across, *stat.shape)).reshape(-1, values), "panel", 0, 0, tiled=True
    ).reshape(across, *stat.shape)
    tops = every[:, : groups + middles]
    top_all = jnp.max(tops, axis=0)
    shifts = jnp.exp(tops - top_all[None])
    sum_all = jnp.sum(every[:, groups + middles :] * shifts[:, :groups], axis=0)

    def shift(px, py):
        return lax.dynamic_slice(shifts, (px * 4 + py, 0, 0), (1, groups + middles, values))[0]

    shift_own = shift(x, y)
    shift_x = {d: shift(at(x, d), y)[:groups] for d in (1, -1)}
    shift_y = {d: shift(x, at(y, d))[:groups] for d in (1, -1)}
    e_all3, e_out3 = rescale(e_loc, shift_own[:groups], scale)
    spot = jnp.stack([x, y]).astype(jnp.int32)
    e_mid_tab = mid_loc * shift_own[groups:, None, :]

    w4 = weight_grand.reshape(groups, 4, 4, width, width)

    far = [(0, 2, 0), (1, 2, 0), (0, 2, 1), (1, 2, 1)]
    raw = [(0, 1, 1), (1, 1, 1), (0, -1, 0), (1, -1, 0)]
    passed = [(0, 1, 0), (1, 1, 0), (0, -1, 1), (1, -1, 1)]
    own = [(0, 0, 0), (1, 0, 0), (0, 0, 1), (1, 0, 1)]
    made = dict(zip(far, edge_sums(spot, w4, e_loc3, far)))
    made.update(zip(raw, edge_sums(spot, w4, e_loc3, raw, (made[far[0]],))))
    moves = (MOVE_X, MOVE_Y)
    near_shift = (shift_x, shift_y)
    addends = [moves[g](made[g, 2, h], d) for _, (g, d, h) in enumerate(passed)]
    factors = jnp.stack([near_shift[g][-d][g][None] for g, d, _ in passed])
    plain = {(g, d): moves[g](made[g, d, 1 if d == 1 else 0], d) for g, d, _ in raw}
    sums = dict(zip(passed, edge_sums(spot, w4, e_all3, passed, (made[raw[0]],), addends, factors)))
    got = {(g, d): moves[g](sums[g, d, h], d) for g, d, h in passed}
    made.update(zip(own, edge_sums(spot, w4, e_all3, own, (sums[passed[0]],))))
    def close(g):
        return jnp.concatenate(
            [
                made[g, 0, 0] + plain[g, -1] * near_shift[g][1][g] + got[g, 1],
                made[g, 0, 1] + plain[g, 1] * near_shift[g][-1][g] + got[g, -1],
            ]
        )

    first_x, first_y = close(0), close(1)

    def split(first, base):
        return lambda d: lax.dynamic_slice(first, (at(base, d), 0, 0), (1, *first.shape[1:]))[0]

    s_own = jnp.stack([scatter_direct(MOVE_Y, split(first_x, y)), scatter_direct(MOVE_X, split(first_y, x))])
    norm = jnp.log(sum_all * MEAN_W)
    message = jnp.log(s_own) - norm[:, None, :]

    rows_of = images // values
    pix_late, parent_late = after(pix_grand, first_x), after(parent, first_x)
    tail = [
        jnp.concatenate(
            [
                message[i],
                pix_late[:, i].astype(f32).reshape(rows_of, values),
                jnp.broadcast_to(parent_late[i].astype(f32), (8 - rows_of, values)),
            ]
        )
        for i in range(groups)
    ]
    mine = jnp.stack(tail)
    below, above = MOVE_Z(mine, 1), MOVE_Z(mine, -1)
    swap = lambda v: lax.ppermute(v, "leaf", hop_leaf(0, 1))
    opposite = jnp.stack([MOVE_Z(below[0], 1), MOVE_Z(above[1], -1)])
    near = {(0, 0): mine, (-1, 0): below, (1, 0): above, (2, 0): opposite}
    for d in (0, -1, 1, 2):
        near[d, 1] = swap(near[d, 0])
    mid_tab = after(e_mid_tab, first_x)
    mid_marks = jnp.transpose(after(pix_mid, first_x)).astype(f32)
    wm = root_middle_weight.reshape(middles, 4, 4, roots // 16, width)
    sub = roots // 16

    lines = {}
    x_late, y_late = after(x, first_x), after(y, first_y)
    for h in range(2):
        for d in (0, 1, -1, 2):
            lines[0, d, h] = lax.dynamic_slice(wm[h], (at(x_late, d), 0, 0, 0), (1, 4, sub, width)).reshape(4 * sub, width)
            lines[1, d, h] = lax.dynamic_slice(wm[2 + h], (0, at(y_late, d), 0, 0), (4, 1, sub, width)).reshape(4 * sub, width)
    lines = lax.optimization_barrier(lines)

    stages = [[(0, 0), (0, 1)], [(-1, 0), (1, 0), (-1, 1), (1, 1)], [(2, 0), (2, 1)]]
    notes_of_keys = []
    sums = None
    for keys in stages:
        start, last = keys is stages[0], keys is stages[-1]
        got = children(
            [near[k] for k in keys],
            width,
            images,
            middles,
            before=sums,
            base=base_mid if last else None,
            lines=[lines[g, 2, h] for g in range(2) for h in range(2)] if last else (),
            tables=mid_tab if start else None,
            marks=mid_marks if start else None,
        )
        sums, notes, far_sums = got[:middles], got[middles], got[middles + 1 :]
        if start:
            base_mid = far_sums
        notes_of_keys.append((keys, notes))
    e_mid = sums

    def mid_x(d, h):
        got = far_sums[h] if d == 2 else dot(lines[0, d, h], e_mid[h])
        return got.reshape(4, sub, images)

    def mid_y(d, h):
        got = far_sums[2 + h] if d == 2 else dot(lines[1, d, h], e_mid[2 + h])
        return got.reshape(4, sub, images)

    line_x = ring_scatter(MOVE_X, mid_x)
    line_y = ring_scatter(MOVE_Y, mid_y)

    note_of = {}
    for keys, notes in notes_of_keys:
        notes = after(notes, line_x[0])
        for j, k in enumerate(keys):
            note_of[k] = [notes[groups * j + i] for i in range(groups)]
    zero = after(jnp.int32(0), line_x[0])
    wm_late = [lax.dynamic_index_in_dim(root_middle_weight, zero + u, keepdims=False) for u in range(middles)]

    def pick(parts, base):
        return lambda d: jnp.stack(
            [lax.dynamic_slice(p, (at(base, d), 0, 0), (1, sub, images))[0] for p in parts]
        )

    own_x = scatter_direct(MOVE_Y, pick(line_x, y))
    own_y = scatter_direct(MOVE_X, pick(line_y, x))

    def order(blocks, base):
        out = jnp.stack([blocks[0], blocks[1], blocks[2], blocks[-1]])
        return jnp.roll(out, base, axis=0)

    def fill(first, first_base, second, second_base, block):
        got = gather_direct(first, block)
        rows = [order({d: got[d][h] for d in got}, first_base) for h in range(2)]
        got = ring_gather(second, *rows)
        return [order({d: got[d][h] for d in got}, second_base) for h in range(2)]

    full_x = fill(MOVE_Y, y, MOVE_X, x, own_x)
    full_y = fill(MOVE_X, x, MOVE_Y, y, own_y)
    s_mid = [v.reshape(roots, images) for v in full_x] + [
        jnp.transpose(v, (1, 0, 2, 3)).reshape(roots, images) for v in full_y
    ]

    root_tab = prior[:, None] * jnp.exp(after(emit_root, line_x[0]) + LIFT)
    base = lax.optimization_barrier(dot(root_tab, hot(pix_root, values)))
    p01, p23 = s_mid[0] * s_mid[1], s_mid[2] * s_mid[3]
    t_mid = [base * s_mid[1] * p23, base * s_mid[0] * p23, base * p01 * s_mid[3], base * p01 * s_mid[2]]
    total_own = jnp.sum(base * p01 * p23, axis=0)
    level = after(top_all[:groups] + norm, line_x[0])
    level_own = sum(dot(level, hot(pix_grand[:, i], values), HIGHEST)[i] for i in range(groups))
    tell = jnp.stack([total_own, level_own])
    leaves = lax.axis_size("leaf")
    tell = jnp.sum(
        lax.all_to_all(
            jnp.broadcast_to(tell[None], (leaves, 2, images)).reshape(leaves * 2, images), "leaf", 0, 0, tiled=True
        ).reshape(leaves, 2, images),
        axis=0,
    )
    total = tell[0]
    level_mid = sum(
        dot(after(top_all[groups:], line_x[0]), hot(pix_mid[:, u], values), HIGHEST)[u] for u in range(middles)
    )
    loglik = (jnp.log(total) - LIFT + tell[1] + level_mid) / nodes

    part = 1.0 / total
    q_mid = [
        e_mid[u]
        * part
        * lax.dot_general(wm_late[u], t_mid[u], (((0,), (0,)), ((), ())), precision=HIGH)
        for u in range(middles)
    ]
    flow_mid = jnp.stack(
        [
            wm_late[u] * dot_t(t_mid[u], e_mid[u] * (part * scale))
            for u in range(middles)
        ]
    )

    def grouped(k, i):
        note = note_of[k][i]
        mine = sum(jnp.where(note[1:2] == u, q_mid[u], 0.0) for u in range(middles))
        mark = jnp.arange(values, dtype=jnp.int32).astype(f32)[:, None] == note[0:1]
        return dot_t(mine, mark.astype(f32))

    q_own = {}
    for d in (2, 1, -1, 0):
        away = jnp.stack([grouped((d, 1), i) for i in range(groups)])
        here = jnp.stack([grouped((d, 0), i) for i in range(groups)])
        q_own[d] = here + lax.ppermute(away, "leaf", hop_leaf(0, 1))
    q_sum = ring_scatter(MOVE_Z, lambda d, h: q_own[d][h])
    ratio = [q_sum[i] / s_own[i] for i in range(groups)]


    def ratios(first, first_base, second, block):
        rows = order(gather_direct(first, block), first_base)
        got = ring_gather(second, rows[:2], rows[2:], False)
        return {(d, h): got[d][h] for d in got for h in range(2)}

    r_x = ratios(MOVE_Y, y, MOVE_X, ratio[0])
    r_y = ratios(MOVE_X, x, MOVE_Y, ratio[1])
    flow = None
    for steps in ((0, 1, -1), (2,)):
        keys = [(d, h) for d in steps for h in range(2)]
        for group, held in ((0, r_x), (1, r_y)):
            flow = edge_flows(spot, w4, {k: held[k] for k in keys}, e_out3, group, flow)
    flow_grand = flow.reshape(groups, states, width)
    return (loglik, flow_grand, flow_mid)


def solution(mesh):
    placed = (
        P(None, "leaf"),
        P(),
        P(),
        P("leaf"),
        P("leaf", "panel", None),
        P(None, "panel", None),
        P("leaf", None),
        P("leaf", None, "panel"),
        P(None, "leaf", "panel"),
        P("leaf"),
    )
    return jax.shard_map(
        shards,
        mesh=mesh,
        in_specs=placed,
        out_specs=(P(), P("leaf", None, "panel"), P(None, "leaf", "panel")),
        check_vma=False,
    )
```

```python
import jax
import jax.numpy as jnp
from jax import lax
from jax.experimental import pallas as pl
from jax.experimental.pallas import tpu as pltpu
from jax.sharding import PartitionSpec as P


HIGH = lax.Precision.HIGH
HIGHEST = lax.Precision.HIGHEST
LIFT = 35.0
MEAN_W = 1.09e-4


def ring_x(d):
    return [(x * 4 + y, ((x + d) % 4) * 4 + y) for x in range(4) for y in range(4)]


def ring_y(d):
    return [(x * 4 + y, x * 4 + (y + d) % 4) for x in range(4) for y in range(4)]


def ring_z(d):
    return [(z * 2 + c, ((z + d) % 4) * 2 + c) for z in range(4) for c in range(2)]


def hop_leaf(d, flip):
    return [(z * 2 + c, ((z + d) % 4) * 2 + (c ^ flip)) for z in range(4) for c in range(2)]


def mover(axis, ring):
    return lambda v, d: lax.ppermute(v, axis, ring(d))


MOVE_X = mover("panel", ring_x)
MOVE_Y = mover("panel", ring_y)
MOVE_Z = mover("leaf", ring_z)


def ring_scatter(move, piece, scale=None, merged=True):
    if scale is None:
        scale = lambda v, d: v
        common = piece
    else:
        common = lambda d, h: piece(d, h, True)
    r1 = move(piece(2, 0), 1)
    r2 = move(piece(2, 1), -1)
    if merged:
        up = move(jnp.stack([common(1, 0) + scale(r1, -1), common(1, 1)]), 1)
        down = move(jnp.stack([common(-1, 0), common(-1, 1) + scale(r2, 1)]), -1)
        return common(0, 0) + up[0] + down[0], common(0, 1) + up[1] + down[1]
    r3 = move(piece(1, 1), 1)
    r4 = move(piece(-1, 0), -1)
    sums = common(1, 0) + scale(r1, -1), common(-1, 1) + scale(r2, 1)
    r5, r6 = move(sums[0], 1), move(sums[1], -1)
    return sums, lambda own0, own1: (own0 + scale(r4, 1) + r5, own1 + scale(r3, -1) + r6)


def ring_gather(move, half0, half1, merged=True):
    if merged:
        both = jnp.stack([half0, half1])
        a, b = move(both, 1), move(both, -1)
        return {0: (half0, half1), -1: (a[0], a[1]), 1: (b[0], b[1]), 2: (move(a[0], 1), move(b[1], -1))}
    a1 = move(half0, 1)
    b2 = move(half1, -1)
    b1 = move(half1, 1)
    a2 = move(half0, -1)
    a3 = move(a1, 1)
    b3 = move(b2, -1)
    return {0: (half0, half1), -1: (a1, b1), 1: (a2, b2), 2: (a3, b3)}


def scatter_direct(move, piece):
    return piece(0) + move(piece(1), 1) + move(piece(-1), -1) + move(piece(2), 2)


def gather_direct(move, block):
    return {0: block, -1: move(block, 1), 1: move(block, -1), 2: move(block, 2)}


def prepare(emit_grand, emit_mid):
    groups, width, values = emit_grand.shape
    middles = emit_mid.shape[0]

    def kernel(grand_ref, mid_ref, e_ref, e3_ref, m_ref, stat_ref):
        for i in range(groups):
            top = jnp.max(grand_ref[i], axis=0, keepdims=True)
            e = jnp.exp(grand_ref[i] - top)
            e_ref[i] = e
            put_triple(e3_ref, i, e)
            stat_ref[i : i + 1, :] = top
            stat_ref[groups + middles + i : groups + middles + i + 1, :] = jnp.sum(e, axis=0, keepdims=True)
        for i in range(middles):
            top = jnp.max(mid_ref[i], axis=0, keepdims=True)
            m_ref[i] = jnp.exp(mid_ref[i] - top)
            stat_ref[groups + i : groups + i + 1, :] = top

    return pl.pallas_call(
        kernel,
        out_shape=(
            jax.ShapeDtypeStruct(emit_grand.shape, jnp.float32),
            jax.ShapeDtypeStruct((groups, 3 * width, values), jnp.bfloat16),
            jax.ShapeDtypeStruct(emit_mid.shape, jnp.float32),
            jax.ShapeDtypeStruct((2 * groups + middles, values), jnp.float32),
        ),
        name="prepare",
    )(emit_grand, emit_mid)


def halves(v):
    high = v.astype(jnp.bfloat16)
    return high, (v - high.astype(jnp.float32)).astype(jnp.bfloat16)


def prepare(emit_grand, emit_mid):
    groups, width, values = emit_grand.shape
    middles = emit_mid.shape[0]

    def kernel(grand_ref, mid_ref, e_ref, e3_ref, m_ref, stat_ref):
        for i in range(groups):
            top = jnp.max(grand_ref[i], axis=0, keepdims=True)
            e = jnp.exp(grand_ref[i] - top)
            e_ref[i] = e
            put_triple(e3_ref, i, e)
            stat_ref[i : i + 1, :] = top
            stat_ref[groups + middles + i : groups + middles + i + 1, :] = jnp.sum(e, axis=0, keepdims=True)
        for i in range(middles):
            top = jnp.max(mid_ref[i], axis=0, keepdims=True)
            m_ref[i] = jnp.exp(mid_ref[i] - top)
            stat_ref[groups + i : groups + i + 1, :] = top

    return pl.pallas_call(
        kernel,
        out_shape=(
            jax.ShapeDtypeStruct(emit_grand.shape, jnp.float32),
            jax.ShapeDtypeStruct((groups, 3 * width, values), jnp.bfloat16),
            jax.ShapeDtypeStruct(emit_mid.shape, jnp.float32),
            jax.ShapeDtypeStruct((2 * groups + middles, values), jnp.float32),
        ),
        name="prepare",
    )(emit_grand, emit_mid)


def put_triple(ref, i, b):
    high, low = halves(b)
    rows = b.shape[0]
    ref[i, :rows] = high
    ref[i, rows : 2 * rows] = high
    ref[i, 2 * rows :] = low


def deep(a, b3):
    high, low = halves(a)
    return jnp.dot(jnp.concatenate([high, low, high], axis=1), b3, preferred_element_type=jnp.float32)


def rescale(e, shift, scale):
    groups, width, values = e.shape

    def kernel(e_ref, shift_ref, up_ref, down_ref):
        for i in range(groups):
            moved = e_ref[i] * shift_ref[i : i + 1, :]
            put_triple(up_ref, i, moved)
            put_triple(down_ref, i, jnp.transpose(moved * scale))

    return pl.pallas_call(
        kernel,
        out_shape=(
            jax.ShapeDtypeStruct((groups, 3 * width, values), jnp.bfloat16),
            jax.ShapeDtypeStruct((groups, 3 * values, width), jnp.bfloat16),
        ),
        name="rescale",
    )(e, shift)


def block_of(ref, spot_ref, group, d, h):
    line = lax.rem(spot_ref[group] + (d + 4), 4)
    if group == 0:
        return ref.at[0, line, pl.ds(2 * h, 2)]
    return ref.at[1, pl.ds(2 * h, 2), line]


ANY = pl.BlockSpec(memory_space=pl.ANY)


def edge_sums(spot, w4, e3, pieces, deps=(), addends=(), factors=None):
    width, values = w4.shape[-1], e3.shape[-1]
    count, waits, more = len(pieces), len(deps), len(addends)
    rows = [] if factors is None else [factors]

    def kernel(spot_ref, w_ref, e_ref, *refs):
        add_refs, refs = refs[waits : waits + more], refs[waits + more :]
        row_refs, refs = refs[: len(rows)], refs[len(rows) :]
        out_refs = refs[:count]
        w_buf, out_buf, in_sem, out_sem, *add = refs[count:]
        for k in range(more):
            pltpu.make_async_copy(add_refs[k], add[0].at[k], add[1].at[k]).start()
        for k, (group, d, h) in enumerate(pieces):
            pltpu.make_async_copy(block_of(w_ref, spot_ref, group, d, h), w_buf.at[k], in_sem.at[k]).start()
        outs = [pltpu.make_async_copy(out_buf.at[k], out_refs[k], out_sem.at[k]) for k in range(count)]

        @pl.loop(0, count)
        def _(k):
            pltpu.make_async_copy(w_ref.at[0, 0, pl.ds(0, 2)], w_buf.at[k], in_sem.at[k]).wait()
            got = deep(w_buf[k].reshape(2 * width, width), e_ref[lax.rem(k, 2)])
            got = got.reshape(2, width, values)
            if more:
                pltpu.make_async_copy(add_refs[0], add[0].at[k], add[1].at[k]).wait()
                got = got + add[0][k] * row_refs[0][k]
            out_buf[k] = got
            for j in range(count):
                pl.when(k == j)(outs[j].start)

        for copy in outs:
            copy.wait()

    return pl.pallas_call(
        kernel,
        in_specs=[pl.BlockSpec(memory_space=pltpu.SMEM), ANY, pl.BlockSpec(memory_space=pltpu.VMEM)]
        + [ANY] * (waits + more)
        + [pl.BlockSpec(memory_space=pltpu.VMEM)] * len(rows),
        out_specs=[ANY] * count,
        out_shape=[jax.ShapeDtypeStruct((2, width, values), jnp.float32)] * count,
        scratch_shapes=[
            pltpu.VMEM((count, 2, width, width), jnp.float32),
            pltpu.VMEM((count, 2, width, values), jnp.float32),
            pltpu.SemaphoreType.DMA((count,)),
            pltpu.SemaphoreType.DMA((count,)),
        ]
        + ([pltpu.VMEM((count, 2, width, values), jnp.float32), pltpu.SemaphoreType.DMA((count,))] if more else []),
        cost_estimate=pl.CostEstimate(
            flops=12 * count * width * width * values,
            bytes_accessed=16 * count * width * width,
            transcendentals=0,
        ),
        name="edge_sums",
    )(spot, w4, e3, *deps, *addends, *rows)


def children(blocks, width, images, middles, before=None, base=None, lines=(), tables=None, marks=None):
    values = blocks[0].shape[-1]
    lead = [] if before is None else list(before)
    lines = list(lines)
    looked = [] if tables is None else [tables, marks]
    last = [] if base is None else list(base)

    def kernel(*refs):
        block_refs = refs[: len(blocks)]
        lead_refs = refs[len(blocks) : len(blocks) + len(lead)]
        last_refs = refs[len(blocks) + len(lead) : len(blocks) + len(lead) + len(last)]
        ends = len(blocks) + len(lead) + len(last)
        line_refs = refs[ends : ends + len(lines)]
        ends += len(lines)
        look_refs = refs[ends : ends + len(looked)]
        ends += len(looked)
        out_refs, note_ref = refs[ends : ends + middles], refs[ends + middles]
        sum_refs = refs[ends + middles + 1 :]
        for u in range(middles if looked else 0):
            ids = lax.broadcasted_iota(jnp.int32, (values, images), 0).astype(jnp.float32)
            mark = (ids == look_refs[1][u : u + 1, :]).astype(jnp.bfloat16)
            high, low = halves(look_refs[0][u])
            sum_refs[u][...] = jnp.dot(
                jnp.concatenate([high, low], axis=1),
                jnp.concatenate([mark, mark], axis=0),
                preferred_element_type=jnp.float32,
            )
        spot = 0
        for u in range(middles):
            out_refs[u][...] = lead_refs[u][...] if lead else jnp.zeros((width, images), jnp.float32)
        for ref in block_refs:
            for i in range(ref.shape[0]):
                note = ref[i, width:, :]
                ids = lax.broadcasted_iota(jnp.int32, (values, values), 0).astype(jnp.float32)
                parts = images // values
                mark = jnp.concatenate(
                    [(ids == note[r : r + 1, :]).astype(jnp.bfloat16) for r in range(parts)], axis=1
                )
                note_ref[spot, 0:1, :] = jnp.concatenate([note[r : r + 1, :] for r in range(parts)], axis=1)
                note_ref[spot, 1:2, :] = jnp.concatenate([note[parts : parts + 1, :]] * parts, axis=1)
                spot += 1
                high, low = halves(ref[i, :width, :])
                got = jnp.dot(
                    jnp.concatenate([high, low], axis=1),
                    jnp.concatenate([mark, mark], axis=0),
                    preferred_element_type=jnp.float32,
                )
                owner = note[images // values : images // values + 1, :1]
                for u in range(middles):
                    out_refs[u][...] += jnp.where(owner == u, got, 0.0)
        if last:
            for u in range(middles):
                done = last_refs[u][...] * jnp.exp(out_refs[u][...])
                out_refs[u][...] = done
                if lines:
                    high, low = halves(done)
                    sum_refs[u][...] = deep(line_refs[u][...], jnp.concatenate([high, high, low], axis=0))

    return pl.pallas_call(
        kernel,
        out_shape=[jax.ShapeDtypeStruct((width, images), jnp.float32)] * middles
        + [jax.ShapeDtypeStruct((sum(b.shape[0] for b in blocks), 8, images), jnp.float32)]
        + [jax.ShapeDtypeStruct((v.shape[0], images), jnp.float32) for v in lines]
        + [jax.ShapeDtypeStruct((width, images), jnp.float32)] * (middles if looked else 0),
        cost_estimate=pl.CostEstimate(
            flops=4 * sum(b.shape[0] for b in blocks) * width * values * images,
            bytes_accessed=4 * (sum(b.size for b in blocks) + middles * width * images * (1 + bool(lead) + bool(last))),
            transcendentals=0,
        ),
        name="children",
    )(*blocks, *lead, *last, *lines, *looked)


def edge_flows(spot, w4, ratios, e3, before=None):
    width, values = w4.shape[-1], e3.shape[1] // 3
    keys = list(ratios)
    count = len(keys)
    extra = [] if before is None else [before]

    def kernel(spot_ref, w_ref, e_ref, *refs):
        ratio_refs = refs[:count]
        out_ref, w_buf, ratio_buf, out_buf, w_sem, ratio_sem, out_sem = refs[count + len(extra) :]
        for k, (group, d, h) in enumerate(keys):
            pltpu.make_async_copy(ratio_refs[k], ratio_buf.at[k], ratio_sem.at[k]).start()
            pltpu.make_async_copy(block_of(w_ref, spot_ref, group, d, h), w_buf.at[k], w_sem.at[k]).start()
        outs = [
            pltpu.make_async_copy(out_buf.at[k], block_of(out_ref, spot_ref, group, d, h), out_sem.at[k])
            for k, (group, d, h) in enumerate(keys)
        ]

        @pl.loop(0, count)
        def _(k):
            pltpu.make_async_copy(ratio_refs[0], ratio_buf.at[k], ratio_sem.at[k]).wait()
            got = deep(ratio_buf[k].reshape(2 * width, values), e_ref[lax.rem(k, 2)])
            pltpu.make_async_copy(w_ref.at[0, 0, pl.ds(0, 2)], w_buf.at[k], w_sem.at[k]).wait()
            out_buf[k] = w_buf[k] * got.reshape(2, width, width)
            for j in range(count):
                pl.when(k == j)(outs[j].start)

        for copy in outs:
            copy.wait()

    return pl.pallas_call(
        kernel,
        in_specs=[pl.BlockSpec(memory_space=pltpu.SMEM), ANY, pl.BlockSpec(memory_space=pltpu.VMEM)]
        + [ANY] * (count + len(extra)),
        out_specs=ANY,
        out_shape=jax.ShapeDtypeStruct(w4.shape, jnp.float32),
        scratch_shapes=[
            pltpu.VMEM((count, 2, width, width), jnp.float32),
            pltpu.VMEM((count, 2, width, values), jnp.float32),
            pltpu.VMEM((count, 2, width, width), jnp.float32),
            pltpu.SemaphoreType.DMA((count,)),
            pltpu.SemaphoreType.DMA((count,)),
            pltpu.SemaphoreType.DMA((count,)),
        ],
        input_output_aliases={3 + count: 0} if extra else {},
        cost_estimate=pl.CostEstimate(
            flops=12 * count * width * width * values,
            bytes_accessed=24 * count * width * width,
            transcendentals=0,
        ),
        name="edge_flows",
    )(spot, w4, e3, *[ratios[k] for k in keys], *extra)


def after(v, array):
    return v + (0.0 * array[(0,) * array.ndim]).astype(v.dtype)


def hot(pixels, values):
    return (jnp.arange(values, dtype=jnp.int32)[:, None] == pixels[None, :]).astype(jnp.float32)


def dot(a, b, precision=HIGH):
    return jnp.dot(a, b, precision=precision)


def dot_t(a, b, precision=HIGH):
    return lax.dot_general(a, b, (((1,), (1,)), ((), ())), precision=precision)


def shards(
    pix_grand,
    pix_mid,
    pix_root,
    parent,
    emit_grand,
    emit_mid,
    emit_root,
    weight_grand,
    root_middle_weight,
    prior,
):
    f32 = jnp.float32
    images = pix_grand.shape[0]
    groups, states, width = weight_grand.shape
    middles, roots, _ = root_middle_weight.shape
    values = emit_root.shape[1]
    scale = states * states / images
    nodes = groups * lax.axis_size("leaf") + middles + 1
    place = lax.axis_index("panel")
    x, y = place // 4, place % 4

    def at(base, d):
        return (base + d + 4) % 4

    e_loc, e_loc3, mid_loc, stat = prepare(emit_grand, emit_mid)
    top_own = stat[: groups + middles]

    across = lax.axis_size("panel")
    every = lax.all_to_all(
        jnp.broadcast_to(stat[None], (across, *stat.shape)).reshape(-1, values), "panel", 0, 0, tiled=True
    ).reshape(across, *stat.shape)
    tops = every[:, : groups + middles]
    top_all = jnp.max(tops, axis=0)
    shifts = jnp.exp(tops - top_all[None])
    sum_all = jnp.sum(every[:, groups + middles :] * shifts[:, :groups], axis=0)

    def shift(px, py):
        return lax.dynamic_slice(shifts, (px * 4 + py, 0, 0), (1, groups + middles, values))[0]

    shift_own = shift(x, y)
    shift_x = {d: shift(at(x, d), y)[:groups] for d in (1, -1)}
    shift_y = {d: shift(x, at(y, d))[:groups] for d in (1, -1)}
    e_all3, e_out3 = rescale(e_loc, shift_own[:groups], scale)
    spot = jnp.stack([x, y]).astype(jnp.int32)
    e_mid_tab = mid_loc * shift_own[groups:, None, :]

    w4 = weight_grand.reshape(groups, 4, 4, width, width)

    far = [(0, 2, 0), (1, 2, 0), (0, 2, 1), (1, 2, 1)]
    raw = [(0, 1, 1), (1, 1, 1), (0, -1, 0), (1, -1, 0)]
    passed = [(0, 1, 0), (1, 1, 0), (0, -1, 1), (1, -1, 1)]
    own = [(0, 0, 0), (1, 0, 0), (0, 0, 1), (1, 0, 1)]
    made = dict(zip(far, edge_sums(spot, w4, e_loc3, far)))
    made.update(zip(raw, edge_sums(spot, w4, e_loc3, raw, (made[far[0]],))))
    moves = (MOVE_X, MOVE_Y)
    near_shift = (shift_x, shift_y)
    addends = [moves[g](made[g, 2, h], d) for _, (g, d, h) in enumerate(passed)]
    factors = jnp.stack([near_shift[g][-d][g][None] for g, d, _ in passed])
    plain = {(g, d): moves[g](made[g, d, 1 if d == 1 else 0], d) for g, d, _ in raw}
    sums = dict(zip(passed, edge_sums(spot, w4, e_all3, passed, (made[raw[0]],), addends, factors)))
    got = {(g, d): moves[g](sums[g, d, h], d) for g, d, h in passed}
    made.update(zip(own, edge_sums(spot, w4, e_all3, own, (sums[passed[0]],))))
    def close(g):
        return jnp.concatenate(
            [
                made[g, 0, 0] + plain[g, -1] * near_shift[g][1][g] + got[g, 1],
                made[g, 0, 1] + plain[g, 1] * near_shift[g][-1][g] + got[g, -1],
            ]
        )

    first_x, first_y = close(0), close(1)

    def split(first, base):
        return lambda d: lax.dynamic_slice(first, (at(base, d), 0, 0), (1, *first.shape[1:]))[0]

    s_own = jnp.stack([scatter_direct(MOVE_Y, split(first_x, y)), scatter_direct(MOVE_X, split(first_y, x))])
    norm = jnp.log(sum_all * MEAN_W)
    message = jnp.log(s_own) - norm[:, None, :]

    rows_of = images // values
    pix_late, parent_late = after(pix_grand, first_x), after(parent, first_x)
    tail = [
        jnp.concatenate(
            [
                message[i],
                pix_late[:, i].astype(f32).reshape(rows_of, values),
                jnp.broadcast_to(parent_late[i].astype(f32), (8 - rows_of, values)),
            ]
        )
        for i in range(groups)
    ]
    mine = jnp.stack(tail)
    below, above = MOVE_Z(mine, 1), MOVE_Z(mine, -1)
    swap = lambda v: lax.ppermute(v, "leaf", hop_leaf(0, 1))
    opposite = jnp.stack([MOVE_Z(below[0], 1), MOVE_Z(above[1], -1)])
    near = {(0, 0): mine, (-1, 0): below, (1, 0): above, (2, 0): opposite}
    for d in (0, -1, 1, 2):
        near[d, 1] = swap(near[d, 0])
    mid_tab = after(e_mid_tab, first_x)
    mid_marks = jnp.transpose(after(pix_mid, first_x)).astype(f32)
    wm = root_middle_weight.reshape(middles, 4, 4, roots // 16, width)
    sub = roots // 16

    lines = {}
    x_late, y_late = after(x, first_x), after(y, first_y)
    for h in range(2):
        for d in (0, 1, -1, 2):
            lines[0, d, h] = lax.dynamic_slice(wm[h], (at(x_late, d), 0, 0, 0), (1, 4, sub, width)).reshape(4 * sub, width)
            lines[1, d, h] = lax.dynamic_slice(wm[2 + h], (0, at(y_late, d), 0, 0), (4, 1, sub, width)).reshape(4 * sub, width)
    lines = lax.optimization_barrier(lines)

    stages = [[(0, 0), (0, 1)], [(-1, 0), (1, 0), (-1, 1), (1, 1)], [(2, 0), (2, 1)]]
    notes_of_keys = []
    sums = None
    for keys in stages:
        start, last = keys is stages[0], keys is stages[-1]
        got = children(
            [near[k] for k in keys],
            width,
            images,
            middles,
            before=sums,
            base=base_mid if last else None,
            lines=[lines[g, 2, h] for g in range(2) for h in range(2)] if last else (),
            tables=mid_tab if start else None,
            marks=mid_marks if start else None,
        )
        sums, notes, far_sums = got[:middles], got[middles], got[middles + 1 :]
        if start:
            base_mid = far_sums
        notes_of_keys.append((keys, notes))
    e_mid = sums

    def mid_x(d, h):
        got = far_sums[h] if d == 2 else dot(lines[0, d, h], e_mid[h])
        return got.reshape(4, sub, images)

    def mid_y(d, h):
        got = far_sums[2 + h] if d == 2 else dot(lines[1, d, h], e_mid[2 + h])
        return got.reshape(4, sub, images)

    line_x = ring_scatter(MOVE_X, mid_x)
    line_y = ring_scatter(MOVE_Y, mid_y)

    note_of = {}
    for keys, notes in notes_of_keys:
        notes = after(notes, line_x[0])
        for j, k in enumerate(keys):
            note_of[k] = [notes[groups * j + i] for i in range(groups)]
    zero = after(jnp.int32(0), line_x[0])
    wm_late = [lax.dynamic_index_in_dim(root_middle_weight, zero + u, keepdims=False) for u in range(middles)]

    def pick(parts, base):
        return lambda d: jnp.stack(
            [lax.dynamic_slice(p, (at(base, d), 0, 0), (1, sub, images))[0] for p in parts]
        )

    own_x = scatter_direct(MOVE_Y, pick(line_x, y))
    own_y = scatter_direct(MOVE_X, pick(line_y, x))

    def order(blocks, base):
        out = jnp.stack([blocks[0], blocks[1], blocks[2], blocks[-1]])
        return jnp.roll(out, base, axis=0)

    def fill(first, first_base, second, second_base, block):
        got = gather_direct(first, block)
        rows = [order({d: got[d][h] for d in got}, first_base) for h in range(2)]
        got = ring_gather(second, *rows)
        return [order({d: got[d][h] for d in got}, second_base) for h in range(2)]

    full_x = fill(MOVE_Y, y, MOVE_X, x, own_x)
    full_y = fill(MOVE_X, x, MOVE_Y, y, own_y)
    s_mid = [v.reshape(roots, images) for v in full_x] + [
        jnp.transpose(v, (1, 0, 2, 3)).reshape(roots, images) for v in full_y
    ]

    root_tab = prior[:, None] * jnp.exp(after(emit_root, line_x[0]) + LIFT)
    base = lax.optimization_barrier(dot(root_tab, hot(pix_root, values)))
    p01, p23 = s_mid[0] * s_mid[1], s_mid[2] * s_mid[3]
    t_mid = [base * s_mid[1] * p23, base * s_mid[0] * p23, base * p01 * s_mid[3], base * p01 * s_mid[2]]
    total_own = jnp.sum(base * p01 * p23, axis=0)
    level = after(top_all[:groups] + norm, line_x[0])
    level_own = sum(dot(level, hot(pix_grand[:, i], values), HIGHEST)[i] for i in range(groups))
    tell = jnp.stack([total_own, level_own])
    leaves = lax.axis_size("leaf")
    tell = jnp.sum(
        lax.all_to_all(
            jnp.broadcast_to(tell[None], (leaves, 2, images)).reshape(leaves * 2, images), "leaf", 0, 0, tiled=True
        ).reshape(leaves, 2, images),
        axis=0,
    )
    total = tell[0]
    level_mid = sum(
        dot(after(top_all[groups:], line_x[0]), hot(pix_mid[:, u], values), HIGHEST)[u] for u in range(middles)
    )
    loglik = (jnp.log(total) - LIFT + tell[1] + level_mid) / nodes

    part = 1.0 / total
    q_mid = [
        e_mid[u]
        * part
        * lax.dot_general(wm_late[u], t_mid[u], (((0,), (0,)), ((), ())), precision=HIGH)
        for u in range(middles)
    ]
    flow_mid = jnp.stack(
        [
            wm_late[u] * dot_t(t_mid[u], e_mid[u] * (part * scale))
            for u in range(middles)
        ]
    )

    def grouped(k, i):
        note = note_of[k][i]
        mine = sum(jnp.where(note[1:2] == u, q_mid[u], 0.0) for u in range(middles))
        mark = jnp.arange(values, dtype=jnp.int32).astype(f32)[:, None] == note[0:1]
        return dot_t(mine, mark.astype(f32))

    q_own = {}
    for d in (2, 1, -1, 0):
        away = jnp.stack([grouped((d, 1), i) for i in range(groups)])
        here = jnp.stack([grouped((d, 0), i) for i in range(groups)])
        q_own[d] = here + lax.ppermute(away, "leaf", hop_leaf(0, 1))
    q_sum = ring_scatter(MOVE_Z, lambda d, h: q_own[d][h])
    ratio = [q_sum[i] / s_own[i] for i in range(groups)]


    def ratios(first, first_base, second, block):
        rows = order(gather_direct(first, block), first_base)
        got = ring_gather(second, rows[:2], rows[2:], False)
        return {(d, h): got[d][h] for d in got for h in range(2)}

    r_x = ratios(MOVE_Y, y, MOVE_X, ratio[0])
    r_y = ratios(MOVE_X, x, MOVE_Y, ratio[1])
    flow = None
    for steps in ((0, 1, -1), (2,)):
        keys = [(g, d, h) for d in steps for h in range(2) for g in range(2)]
        flow = edge_flows(spot, w4, {k: (r_x, r_y)[k[0]][k[1:]] for k in keys}, e_out3, flow)
    flow_grand = flow.reshape(groups, states, width)
    return (loglik, flow_grand, flow_mid)


def solution(mesh):
    placed = (
        P(None, "leaf"),
        P(),
        P(),
        P("leaf"),
        P("leaf", "panel", None),
        P(None, "panel", None),
        P("leaf", None),
        P("leaf", None, "panel"),
        P(None, "leaf", "panel"),
        P("leaf"),
    )
    return jax.shard_map(
        shards,
        mesh=mesh,
        in_specs=placed,
        out_specs=(P(), P("leaf", None, "panel"), P(None, "leaf", "panel")),
        check_vma=False,
    )
```
